32 devices in a mesh: pipe: 4 (over y, x), expert: 8 (over z, core).
Axes of the slice: x: 2, y: 2, z: 4, core: 2. Of those that a mesh axis runs over, the one named last changes fastest.
Arguments:
- tokens_in: bfloat16 [2, 640, 2048], P(None, 'expert'), may hold values from -6 to 6
- out_grad: bfloat16 [2, 640, 2048], P(None, 'expert'), may hold values from -6 to 6
- routes: int32 [4, 2, 640, 1], P(None, None, 'expert'), may hold values from 0 to 7; in each aligned block of 80 rows (0 to 79, 80 to 159, ..., all dimensions but the last counted through in order) at most 15 rows name the same one
- router: bfloat16 [4, 2048, 8], P('pipe'), may hold values from -0.125 to 0.125
- norm_gain: bfloat16 [4, 2048], P('pipe'), may hold values from 0.5 to 1.5
- w_in: bfloat16 [4, 8, 2048, 1024], P('pipe', 'expert'), may hold values from -0.125 to 0.125
- w_out: bfloat16 [4, 8, 512, 2048], P('pipe', 'expert'), may hold values from -0.25 to 0.25
Outputs:
- grad_in: bfloat16 [4, 8, 2048, 1024], P('pipe', 'expert')
- grad_out: bfloat16 [4, 8, 512, 2048], P('pipe', 'expert')
The draws below stay inside these ranges and needn't reach their ends.
Inputs may be any that keep to these rules, and one draw needn't show every extreme that they name: `routes`: in each aligned block of 80 rows (one device's tokens of one layer and microbatch) no expert is named by more than 15 tokens; a token's 1 ids differ.
All inputs are finite; a program needn't handle non-finite values.
Results may differ from the reference program's by a relative error of at most 0.029.
Values may be sent and summed in bfloat16 or wider, within the bound.
No kernel may reach another device: no remote copies, remote signals or barrier semaphores. Data moves between devices by JAX's collectives and lax.ppermute only.
A program may use at most 128 MiB of HBM per device.

```python
import math
import jax
import jax.numpy as jnp
import numpy as np
from jax import lax

D = 2048
FW = 512
TOPK = 1
MICRO = 2
TOK_DEV = 80
LAYERS = 4
EXPERTS = 8
TOKENS = 640
CAP = 15
N_EXPERT = 8


def block_levels(stream_key, shape, split, least, largest):
    level = 1.0
    for axis_at, shards_of in split:
        draws = jax.random.uniform(jax.random.fold_in(jax.random.fold_in(stream_key, 6), axis_at), (shards_of,), jnp.float32, least / len(split), largest / len(split))
        level = level * jnp.repeat(jnp.exp(draws), shape[axis_at] // shards_of).reshape((-1,) + (1,) * (len(shape) - 1 - axis_at))
    return level


def shared_out(key, own, number, rows, number_of, top, bound, skew):
    sequence = jax.random.permutation(key, number_of)
    crowded, common = load_shares(number_of, rows * top, bound, skew, True), load_shares(number_of, rows * top, bound, skew, False)
    places = jnp.arange(number_of)

    def named(lengths, turn):
        used = int((lengths > 0).sum())
        fixed = max(1, used // 4)
        passed = fixed + (places - fixed + turn * (used - fixed)) % max(1, number_of - fixed)
        return jnp.zeros((number_of,), jnp.int32).at[sequence[jnp.where(places < fixed, places, passed)]].set(jnp.asarray(lengths, jnp.int32))

    lengths = jnp.where(number % 4 == 0, named(crowded, number // 4), named(common, number - number // 4 - 1))
    mixed = jax.random.permutation(jax.random.fold_in(own, 3), number_of)
    giver, taker = mixed[0:number_of // 2 * 2:2], mixed[1:number_of // 2 * 2:2]
    slack = jnp.minimum(lengths[giver] - 1, bound - lengths[taker]) // 2
    slack = jnp.where((giver == sequence[0]) | (taker == sequence[0]) | (lengths[taker] == 0), 0, jnp.maximum(slack, 0))
    passed = jax.random.randint(jax.random.fold_in(own, 4), (number_of // 2,), 0, 1 << 20) % (slack + 1)
    lengths = lengths.at[giver].add(-passed).at[taker].add(passed)
    labels = jnp.searchsorted(jnp.cumsum(lengths), jnp.arange(rows * top), side="right").astype(jnp.int32)
    listing = labels.reshape(top, rows).T
    listing = listing[jax.random.permutation(jax.random.fold_in(own, 1), rows)]
    turn = jax.random.randint(jax.random.fold_in(own, 2), (rows, 1), 0, top)
    return jnp.take_along_axis(listing, (jnp.arange(top)[None, :] + turn) % top, axis=1)


def load_shares(number_of, total, most, slope, full):
    loads = [(1 << 20) // math.isqrt(grade ** slope) + 1 for grade in range(1, number_of + 1)]
    largest = most if full else min(most, max(-(-total // number_of), total * loads[0] // sum(loads)))
    least = 1 if total - largest >= number_of - 1 else 0
    counts, surplus = [largest] + [least] * (number_of - 1), total - largest - least * (number_of - 1)
    while surplus > 0:
        candidates = [i for i in range(1, number_of) if counts[i] < largest] or [i for i in range(1, number_of) if counts[i] < most]
        mass, left = sum([loads[i] for i in candidates]), surplus
        for i in candidates:
            extra = min(most - counts[i], max(1, left * loads[i] // mass), surplus)
            counts[i] = counts[i] + extra
            surplus = surplus - extra
    return np.array(counts)


def bell_draw(stream_key, shape, scale, bound, split=(), held_as=jnp.bfloat16):
    drawn = scale * jax.random.normal(stream_key, shape, jnp.float32)
    if split:
        drawn = drawn * block_levels(stream_key, shape, split, -0.22, 0.18)
    return jnp.clip(drawn, -bound, bound).astype(held_as)


def setup_inputs(seed: int = 0) -> dict:
    key_list = jax.random.split(jax.random.key(seed), 8)
    tokens_in = bell_draw(key_list[0], (MICRO, TOKENS, D), 1.0, 6.0, ((1, 8),))
    out_grad = bell_draw(key_list[1], (MICRO, TOKENS, D), 1.0, 6.0, ((1, 8),))
    routes_keys = jax.random.split(jax.random.fold_in(key_list[2], 1), LAYERS * MICRO * TOKENS // TOK_DEV)
    routes_turns = jax.random.permutation(jax.random.fold_in(key_list[2], 3), LAYERS * MICRO * TOKENS // TOK_DEV)
    routes = jax.vmap(lambda own, number: shared_out(jax.random.fold_in(key_list[2], 2), own, number, TOK_DEV, EXPERTS, TOPK, CAP, 1))(routes_keys, routes_turns).reshape((LAYERS, MICRO, TOKENS, TOPK))
    router = bell_draw(key_list[3], (LAYERS, D, EXPERTS), D ** -0.5, 0.125, ((0, 4),))
    norm_gain = jnp.clip(1.0 + 0.1 * jax.random.normal(key_list[4], (LAYERS, D), jnp.float32), 0.5, 1.5).astype(jnp.bfloat16)
    w_in = bell_draw(key_list[5], (LAYERS, EXPERTS, D, 2 * FW), D ** -0.5, 0.125, ((0, 4), (1, 8)))
    w_out = bell_draw(key_list[6], (LAYERS, EXPERTS, FW, D), FW ** -0.5, 0.25, ((0, 4), (1, 8)))
    return dict(tokens_in=tokens_in, out_grad=out_grad, routes=routes, router=router, norm_gain=norm_gain, w_in=w_in, w_out=w_out)


epsilon = 1e-06

def normalize(hidden, gain_row):
    values = hidden.astype(jnp.float32)
    inverse = lax.rsqrt(lax.optimization_barrier(jnp.mean(values * values, axis=-1, keepdims=True)) + epsilon)
    scaled = values * inverse
    normed = (scaled * gain_row.astype(jnp.float32)).astype(jnp.bfloat16)
    return (normed, scaled, inverse)

def router_gates(normed, router_cols, route_ids):
    logits_all = jnp.dot(normed, router_cols, preferred_element_type=jnp.float32)
    picked = route_ids[:, :, None] == jnp.arange(router_cols.shape[1], dtype=jnp.int32)[None, None, :]
    logits = lax.optimization_barrier(jnp.sum(jnp.where(picked, logits_all[:, None, :], 0.0), axis=-1))
    return (jax.nn.sigmoid(logits), picked)

def slot_owners(positions, slot_count):
    pair_count = positions.shape[0]
    owners = jnp.zeros((slot_count,), jnp.int32).at[positions].set(jnp.arange(pair_count, dtype=jnp.int32))
    filled = jnp.zeros((slot_count,), jnp.int32).at[positions].set(1)
    return (owners, filled > 0)

def to_slots(source, index_table, filled, slot_shape):
    gathered = source[index_table]
    mask_shape = (filled.shape[0],) + (1,) * (gathered.ndim - 1)
    chosen = jnp.where(filled.reshape(mask_shape), gathered, jnp.zeros((), source.dtype))
    return chosen.reshape(slot_shape)

def expert_forward(token_rows, weight_in, weight_out):
    inner_width = weight_out.shape[0]
    joined = jnp.dot(token_rows, weight_in, preferred_element_type=jnp.float32)
    gate_part = joined[:, :inner_width]
    activated = (gate_part * jax.nn.sigmoid(gate_part) * joined[:, inner_width:]).astype(jnp.bfloat16)
    return jnp.dot(activated, weight_out, preferred_element_type=jnp.float32).astype(jnp.bfloat16)

def expert_backward(token_rows, upstream, gate_share, weight_in, weight_out):
    inner_width = weight_out.shape[0]
    joined = jnp.dot(token_rows, weight_in, preferred_element_type=jnp.float32)
    gate_part = joined[:, :inner_width]
    up_part = joined[:, inner_width:]
    sigmoid_gate = jax.nn.sigmoid(gate_part)
    silu_gate = gate_part * sigmoid_gate
    activated = (silu_gate * up_part).astype(jnp.bfloat16)
    produced = jnp.dot(activated, weight_out, preferred_element_type=jnp.float32).astype(jnp.bfloat16)
    upstream_f = upstream.astype(jnp.float32)
    share_grad = lax.optimization_barrier(jnp.sum(produced.astype(jnp.float32) * upstream_f, axis=-1))
    scaled_grad = (gate_share.astype(jnp.float32)[:, None] * upstream_f).astype(jnp.bfloat16)
    act_grad = jnp.dot(scaled_grad, weight_out.T, preferred_element_type=jnp.float32)
    gate_grad = act_grad * up_part * sigmoid_gate * (1.0 + gate_part * (1.0 - sigmoid_gate))
    up_grad = act_grad * silu_gate
    joined_grad = jnp.concatenate([gate_grad, up_grad], axis=-1).astype(jnp.bfloat16)
    rows_grad = jnp.dot(joined_grad, weight_in.T, preferred_element_type=jnp.float32).astype(jnp.bfloat16)
    grad_in = jnp.dot(token_rows.T, joined_grad, preferred_element_type=jnp.float32)
    grad_out = jnp.dot(activated.T, scaled_grad, preferred_element_type=jnp.float32)
    return (rows_grad, share_grad, grad_in, grad_out)

def combine(hidden, gate_probs, pair_outputs):
    shares = lax.optimization_barrier(gate_probs.astype(jnp.bfloat16)).astype(jnp.float32)
    mixed = lax.optimization_barrier(jnp.sum(shares[:, :, None] * pair_outputs.astype(jnp.float32), axis=1))
    return (hidden.astype(jnp.float32) + mixed).astype(jnp.bfloat16)

def token_backward(upstream, scaled, inverse, gain_row, router_cols, gate_probs, picked, pair_grads, pair_shares):
    logit_grad = pair_shares.astype(jnp.float32) * gate_probs * (1.0 - gate_probs)
    spread = lax.optimization_barrier(jnp.sum(jnp.where(picked, logit_grad[:, :, None], 0.0), axis=1))
    normed_grad = lax.optimization_barrier(jnp.sum(pair_grads.astype(jnp.float32), axis=1)) + jnp.dot(spread, router_cols.astype(jnp.float32).T, precision=lax.Precision.HIGHEST)
    gained = normed_grad * gain_row.astype(jnp.float32)
    centred = gained - scaled * lax.optimization_barrier(jnp.mean(gained * scaled, axis=-1, keepdims=True))
    return (upstream.astype(jnp.float32) + inverse * centred).astype(jnp.bfloat16)

def positions_of(route_ids):
    blocks = route_ids.reshape(N_EXPERT, TOK_DEV * TOPK)
    pair_marks = (blocks[:, :, None] == jnp.arange(EXPERTS, dtype=jnp.int32)[None, None, :]).astype(jnp.int32)
    earlier = jnp.cumsum(pair_marks, axis=1) - pair_marks
    slot_index = lax.optimization_barrier(jnp.sum(earlier * pair_marks, axis=2))
    block_ids = jnp.arange(N_EXPERT, dtype=jnp.int32)[:, None]
    return (blocks * (N_EXPERT * CAP) + block_ids * CAP + slot_index).reshape(-1)

def reference(tokens_in, out_grad, routes, router, norm_gain, w_in, w_out):
    slot_total = EXPERTS * N_EXPERT * CAP
    row_shape = (EXPERTS, N_EXPERT * CAP, D)
    stored = []
    hidden_all = [tokens_in[micro_index] for micro_index in range(MICRO)]
    for layer_index in range(LAYERS):
        stored.append(hidden_all)
        new_all = []
        for micro_index in range(MICRO):
            hidden = hidden_all[micro_index]
            normed, scaled, inverse = normalize(hidden, norm_gain[layer_index])
            route_ids = routes[layer_index, micro_index]
            gate_probs, picked = router_gates(normed, router[layer_index], route_ids)
            positions = positions_of(route_ids)
            owners, filled = slot_owners(positions, slot_total)
            send_rows = to_slots(normed, owners // TOPK, filled, row_shape)
            produced = lax.map(lambda packed: expert_forward(packed[0], packed[1], packed[2]), (send_rows, w_in[layer_index], w_out[layer_index]))
            pair_outputs = produced.reshape(slot_total, D)[positions].reshape(TOKENS, TOPK, D)
            new_all.append(combine(hidden, gate_probs, pair_outputs))
        hidden_all = new_all
    grads_all = [out_grad[micro_index] for micro_index in range(MICRO)]
    layer_grads_in = []
    layer_grads_out = []
    for layer_index in reversed(range(LAYERS)):
        total_in = jnp.zeros((EXPERTS, D, 2 * FW), jnp.float32)
        total_out = jnp.zeros((EXPERTS, FW, D), jnp.float32)
        lower_all = []
        for micro_index in range(MICRO):
            hidden = stored[layer_index][micro_index]
            upstream = grads_all[micro_index]
            normed, scaled, inverse = normalize(hidden, norm_gain[layer_index])
            route_ids = routes[layer_index, micro_index]
            gate_probs, picked = router_gates(normed, router[layer_index], route_ids)
            positions = positions_of(route_ids)
            owners, filled = slot_owners(positions, slot_total)
            send_rows = to_slots(normed, owners // TOPK, filled, row_shape)
            send_grad = to_slots(upstream, owners // TOPK, filled, row_shape)
            send_share = to_slots(gate_probs.astype(jnp.bfloat16).reshape(-1), owners, filled, (EXPERTS, N_EXPERT * CAP))
            rows_grad, share_grad, grad_in, grad_out = lax.map(lambda packed: expert_backward(packed[0], packed[1], packed[2], packed[3], packed[4]), (send_rows, send_grad, send_share, w_in[layer_index], w_out[layer_index]))
            total_in = total_in + grad_in
            total_out = total_out + grad_out
            pair_grads = rows_grad.reshape(slot_total, D)[positions].reshape(TOKENS, TOPK, D)
            share_round = lax.optimization_barrier(share_grad.astype(jnp.bfloat16))
            pair_shares = share_round.reshape(slot_total)[positions].reshape(TOKENS, TOPK)
            lower_all.append(token_backward(upstream, scaled, inverse, norm_gain[layer_index], router[layer_index], gate_probs, picked, pair_grads, pair_shares))
        grads_all = lower_all
        layer_grads_in.append(total_in)
        layer_grads_out.append(total_out)
    return (jnp.stack(layer_grads_in[::-1]).astype(jnp.bfloat16), jnp.stack(layer_grads_out[::-1]).astype(jnp.bfloat16))
```

```python
import jax
import jax.numpy as jnp
from jax import lax
from jax.sharding import PartitionSpec as P

epsilon = 1e-06


def normalize(hidden, gain_row):
    values = hidden.astype(jnp.float32)
    inverse = lax.rsqrt(jnp.mean(values * values, axis=-1, keepdims=True) + epsilon)
    scaled = values * inverse
    normed = (scaled * gain_row.astype(jnp.float32)).astype(jnp.bfloat16)
    return (normed, scaled, inverse)


def expert_forward(hidden, gain_row, gate_column, weight_in, weight_out):
    inner_width = weight_out.shape[0]
    normed, _, _ = normalize(hidden, gain_row)
    logits = jnp.sum(normed.astype(jnp.float32) * gate_column, axis=-1, keepdims=True)
    gate = jax.nn.sigmoid(logits)
    joined = jnp.dot(normed, weight_in, preferred_element_type=jnp.float32)
    gate_part = joined[:, :inner_width]
    activated = (gate_part * jax.nn.sigmoid(gate_part) * joined[:, inner_width:]).astype(
        jnp.bfloat16
    )
    produced = jnp.dot(activated, weight_out, preferred_element_type=jnp.float32).astype(
        jnp.bfloat16
    )
    share = gate.astype(jnp.bfloat16).astype(jnp.float32)
    output = (hidden.astype(jnp.float32) + share * produced.astype(jnp.float32)).astype(
        jnp.bfloat16
    )
    return output, (hidden, gate, joined, produced)


def expert_backward(upstream, saved, gain_row, gate_column, weight_in, weight_out):
    hidden, gate, joined, produced = saved
    inner_width = weight_out.shape[0]
    gain = gain_row.astype(jnp.float32)
    normed, scaled, inverse = normalize(hidden, gain_row)
    gate_part = joined[:, :inner_width]
    up_part = joined[:, inner_width:]
    sigmoid_gate = jax.nn.sigmoid(gate_part)
    silu_gate = gate_part * sigmoid_gate
    activated = (silu_gate * up_part).astype(jnp.bfloat16)
    upstream_f = upstream.astype(jnp.float32)
    share_grad = (
        jnp.sum(produced.astype(jnp.float32) * upstream_f, axis=-1, keepdims=True)
        .astype(jnp.bfloat16)
        .astype(jnp.float32)
    )
    share = gate.astype(jnp.bfloat16).astype(jnp.float32)
    scaled_grad = (share * upstream_f).astype(jnp.bfloat16)
    contract_last = (((1,), (1,)), ((), ()))
    act_grad = lax.dot_general(
        scaled_grad, weight_out, contract_last, preferred_element_type=jnp.float32
    )
    gate_grad = act_grad * up_part * sigmoid_gate * (1.0 + gate_part * (1.0 - sigmoid_gate))
    up_grad = act_grad * silu_gate
    joined_grad = jnp.concatenate([gate_grad, up_grad], axis=-1).astype(jnp.bfloat16)
    rows_grad = lax.dot_general(
        joined_grad, weight_in, contract_last, preferred_element_type=jnp.float32
    ).astype(jnp.bfloat16)
    normed_grad = rows_grad.astype(jnp.float32) + share_grad * gate * (1.0 - gate) * gate_column
    gained = normed_grad * gain
    centred = gained - scaled * jnp.mean(gained * scaled, axis=-1, keepdims=True)
    passed = (upstream_f + inverse * centred).astype(jnp.bfloat16)
    return passed, (normed, joined_grad, activated, scaled_grad)


def weight_grads(rows, joined_grad, activated, scaled_grad):
    contract = (((0,), (0,)), ((), ()))
    grad_in = lax.dot_general(rows, joined_grad, contract, preferred_element_type=jnp.float32)
    grad_out = lax.dot_general(activated, scaled_grad, contract, preferred_element_type=jnp.float32)
    return (grad_in.astype(jnp.bfloat16)[None, None], grad_out.astype(jnp.bfloat16)[None, None])


def slot_marks(route_ids, rank, rank_count, width, paired):
    experts = jnp.arange(rank_count, dtype=jnp.int32)
    marks = (route_ids[:, None] == experts[None, :]).astype(jnp.int32)
    earlier = jnp.cumsum(marks, axis=0) - marks
    within = jnp.sum(earlier * marks, axis=1)
    places = route_ids
    if paired:
        offsets = route_ids ^ rank
        places = (offsets % 2) * (rank_count // 2) + offsets // 2
    slots = places * width + within
    return (jnp.arange(rank_count * width, dtype=jnp.int32)[:, None] == slots[None, :]).astype(
        jnp.bfloat16
    )


def shards(tokens_in, out_grad, routes, router, norm_gain, w_in, w_out):
    layers = lax.axis_size("pipe")
    ranks = lax.axis_size("expert")
    layer = lax.axis_index("pipe")
    rank = lax.axis_index("expert")
    micros, tokens, width = tokens_in.shape
    top_count = routes.shape[3]
    assert top_count == 1 and router.shape[2] == ranks and micros <= 2 and layers % 2 == 0
    capacity = max(2, tokens * top_count * 3 // (2 * ranks))
    room = -(-capacity // 8) * 8 if capacity >= 8 else -(-capacity // 4) * 4
    rows = ranks * room
    groups = ranks // 2
    paired = ranks <= 8 and ranks & (ranks - 1) == 0
    last = layers - 1
    own_in, own_out, gain_row = w_in[0, 0], w_out[0, 0], norm_gain
    gate_column = (
        lax.dynamic_index_in_dim(router[0], rank, 1, keepdims=False)
        .astype(jnp.float32)
        .reshape(1, width)
    )

    def marks_of(which_layer, which_micro):
        which_layer = jnp.clip(which_layer, 0, last)
        which_micro = jnp.clip(which_micro, 0, micros - 1)
        ids = lax.dynamic_slice(
            routes, (which_layer, which_micro, 0, 0), (1, 1, tokens, 1)
        ).reshape(tokens)
        return slot_marks(ids, rank, ranks, room, paired)

    def resort(step):
        forward_micro = step - layer
        is_forward = (forward_micro >= 0) & (forward_micro < micros)
        backward_micro = step - (2 * last - layer)
        source_layer = jnp.where(is_forward, layer - 1, layer + 1)
        micro = jnp.where(is_forward, forward_micro, backward_micro)
        here, there = marks_of(layer, micro), marks_of(source_layer, micro)
        return jnp.dot(here, there.T, preferred_element_type=jnp.float32).astype(jnp.bfloat16)

    def permuted(piece, offset, jump):
        route = []
        for p in range(layers):
            q = p if jump is None else jump(p)
            route += [(p * ranks + i, q * ranks + (i ^ offset)) for i in range(ranks)]
        return lax.ppermute(piece, ("pipe", "expert"), route)

    def exchange(pieces, jump):
        if not paired:
            arrived = lax.all_to_all(
                pieces.reshape(ranks, room, width), "expert", split_axis=0, concat_axis=0, tiled=True
            ).reshape(rows, width)
            if jump is None:
                return arrived
            return lax.ppermute(arrived, "pipe", [(p, jump(p)) for p in range(layers)])
        half = rows // 2
        swapped = permuted(pieces[half:], 1, None)
        arrived = [None] * groups
        for k in reversed(range(groups)):
            part = slice(k * room, (k + 1) * room)
            piece = jnp.concatenate([pieces[part], swapped[part]], axis=0)
            arrived[k] = piece if k == 0 and jump is None else permuted(piece, 2 * k, jump)
        return jnp.concatenate([a[:room] for a in arrived] + [a[room:] for a in arrived], axis=0)

    outer = (layer == 0) | (layer == last)
    entering = jnp.where(layer == 0, tokens_in, out_grad)
    steps = 2 * last + micros
    arrivals, forwards, records = [], [], []
    home = None
    kept = tuple(
        jnp.zeros((micros + 1, rows, size), jnp.bfloat16)
        for size in (width, own_in.shape[1], own_out.shape[0], width)
    )
    for step in range(steps):
        if step < micros:
            start = jnp.dot(
                marks_of(layer, step), entering[step], preferred_element_type=jnp.float32
            ).astype(jnp.bfloat16)
        if step > 0:
            sorted_rows = jnp.dot(
                resort(step), home, preferred_element_type=jnp.float32
            ).astype(jnp.bfloat16)
            if step < micros:
                sorted_rows = jnp.where(outer, start, sorted_rows)
        else:
            sorted_rows = start
        arrived = exchange(sorted_rows, None)
        arrivals.append(arrived)
        output = None
        if step < last + micros:
            output, saved = expert_forward(arrived, gain_row, gate_column, own_in, own_out)
            forwards.append(saved)
        if step >= last:
            upstream = arrived
            if step < last + micros:
                upstream = jnp.where(layer == last, arrivals[step - last], arrived)
            saved = forwards[min(len(forwards) - 1, step)]
            for p in range(layers):
                at = step - 2 * last + 2 * p
                if 0 <= at - p < micros:
                    saved = jax.tree.map(
                        lambda one, other: jnp.where(layer == p, one, other), forwards[at], saved
                    )
            passed, record = expert_backward(
                upstream, saved, gain_row, gate_column, own_in, own_out
            )
            micro = step - (2 * last - layer)
            place = jnp.where((micro >= 0) & (micro < micros), micro, micros)
            kept = tuple(
                lax.dynamic_update_index_in_dim(buffer, value, place, 0)
                for buffer, value in zip(kept, record)
            )
            output = jnp.where(layer == last, passed, output) if step == last else passed
        if step < last:
            jump = lambda p: (p + 1) % layers
        elif step == last:
            jump = lambda p: p ^ 1
        else:
            jump = lambda p: (p - 1) % layers
        if step + 1 < steps:
            home = exchange(output, jump)
    return weight_grads(*[buffer[:micros].reshape(micros * rows, -1) for buffer in kept])


def solution(mesh):
    placed = (
        P(None, "expert", None),
        P(None, "expert", None),
        P(None, None, "expert", None),
        P("pipe", None, None),
        P("pipe", None),
        P("pipe", "expert", None, None),
        P("pipe", "expert", None, None),
    )
    return jax.shard_map(
        shards,
        mesh=mesh,
        in_specs=placed,
        out_specs=(P("pipe", "expert", None, None), P("pipe", "expert", None, None)),
        check_vma=False,
    )
```

```python
import functools

import jax
import jax.numpy as jnp
from jax import lax
from jax.experimental import pallas as pl
from jax.experimental.pallas import tpu as pltpu
from jax.sharding import PartitionSpec as P

epsilon = 1e-06


f32, bf16 = jnp.float32, jnp.bfloat16
VMEM = pl.BlockSpec(memory_space=pltpu.VMEM)
SMEM = pl.BlockSpec(memory_space=pltpu.SMEM)
ANY = pl.BlockSpec(memory_space=pl.ANY)
LAST = (((1,), (1,)), ((), ()))
FIRST = (((0,), (0,)), ((), ()))


def joined_rows(refs):
    parts = [ref[...] for ref in refs]
    return parts[0] if len(parts) == 1 else jnp.concatenate(parts, axis=0)


def split_rows(refs, value):
    size = refs[0].shape[0]
    for k, ref in enumerate(refs):
        ref[...] = value[k * size : (k + 1) * size]


def normalize(hidden, gain):
    values = hidden.astype(f32)
    inverse = lax.rsqrt(jnp.mean(values * values, axis=-1, keepdims=True) + epsilon)
    scaled = values * inverse
    return (scaled * gain).astype(bf16), scaled, inverse


def gate_of(normed, column):
    return jax.nn.sigmoid(jnp.sum(normed.astype(f32) * column, axis=-1, keepdims=True))


def forward_kernel(count, gain_ref, column_ref, in_ref, out_ref, *refs):
    arrived, sent = refs[:count], refs[count : 2 * count]
    hidden_ref, joined_ref, produced_ref = refs[2 * count :]
    inner = out_ref.shape[0]
    hidden = joined_rows(arrived)
    normed, _, _ = normalize(hidden, gain_ref[...].astype(f32))
    share = gate_of(normed, column_ref[...]).astype(bf16).astype(f32)
    joined = jnp.dot(normed, in_ref[...], preferred_element_type=f32)
    gate_part = joined[:, :inner]
    activated = (gate_part * jax.nn.sigmoid(gate_part) * joined[:, inner:]).astype(bf16)
    produced = jnp.dot(activated, out_ref[...], preferred_element_type=f32).astype(bf16)
    output = (hidden.astype(f32) + share * produced.astype(f32)).astype(bf16)
    split_rows(sent, output)
    hidden_ref[...] = hidden
    joined_ref[...] = joined
    produced_ref[...] = produced


def backward_kernel(plan, place_ref, gain_ref, column_ref, in_ref, out_ref, *refs):
    count, layers, micros, step, aliased, passes = plan
    last = layers - 1
    layer = place_ref[0]
    refs = list(refs)
    take = lambda number: [refs.pop(0) for _ in range(number)]
    arrived = take(count)
    entered = take(count) if step < last + micros else None
    own = saved_steps(plan)
    saved = [take(3) for _ in own]
    if aliased:
        take(4)
    sent = take(count) if passes else None
    kept = take(4)
    stage = take(4)
    sems = refs.pop(0)
    upstream = joined_rows(arrived)
    if entered is not None:
        upstream = jnp.where(layer == last, joined_rows(entered), upstream)
    upstream_f = upstream.astype(f32)

    def pick(index):
        value = saved[0][index][...]
        for p, group in zip(own[1:], saved[1:]):
            value = jnp.where(layer == p, group[index][...], value)
        return value

    hidden, joined, produced = pick(0), pick(1), pick(2)
    micro = step - (2 * last - layer)
    slot = jnp.where((micro >= 0) & (micro < micros), micro, micros)
    copies = [
        pltpu.make_async_copy(stage[i], kept[i].at[slot], sems.at[i]) for i in range(4)
    ]
    inner = out_ref.shape[0]
    gain, column = gain_ref[...].astype(f32), column_ref[...]
    normed, scaled, inverse = normalize(hidden, gain)
    gate = gate_of(normed, column)
    gate_part, up_part = joined[:, :inner], joined[:, inner:]
    sigmoid_gate = jax.nn.sigmoid(gate_part)
    silu_gate = gate_part * sigmoid_gate
    scaled_grad = (gate.astype(bf16).astype(f32) * upstream_f).astype(bf16)
    stage[0][...] = normed
    stage[2][...] = (silu_gate * up_part).astype(bf16)
    stage[3][...] = scaled_grad
    for i in (0, 2, 3):
        copies[i].start()
    act_grad = lax.dot_general(scaled_grad, out_ref[...], LAST, preferred_element_type=f32)
    gate_grad = act_grad * up_part * sigmoid_gate * (1.0 + gate_part * (1.0 - sigmoid_gate))
    up_grad = act_grad * silu_gate
    joined_grad = jnp.concatenate([gate_grad, up_grad], axis=-1).astype(bf16)
    stage[1][...] = joined_grad
    copies[1].start()
    if passes:
        rows_grad = lax.dot_general(
            joined_grad, in_ref[...], LAST, preferred_element_type=f32
        ).astype(bf16)
        share_grad = jnp.sum(produced.astype(f32) * upstream_f, axis=-1, keepdims=True)
        logit_grad = share_grad.astype(bf16).astype(f32) * gate * (1.0 - gate)
        gained = (rows_grad.astype(f32) + logit_grad * column) * gain
        centred = gained - scaled * jnp.mean(gained * scaled, axis=-1, keepdims=True)
        split_rows(sent, (upstream_f + inverse * centred).astype(bf16))
    for copy in copies:
        copy.wait()


def saved_steps(plan):
    _, layers, micros, step, _, _ = plan
    return [p for p in range(layers) if 0 <= step - (2 * (layers - 1) - p) < micros]


def resort_kernel(plan, place_ref, order_ref, *refs):
    arrivals, count, entry, last = plan
    arrived = refs[:arrivals]
    rest = refs[arrivals:]
    sent = rest[-count:]
    value = jnp.dot(order_ref[0], joined_rows(arrived), preferred_element_type=f32).astype(bf16)
    if entry:
        layer = place_ref[0]
        value = jnp.where((layer == 0) | (layer == last), rest[0][...], value)
    split_rows(sent, value)


def prepare_kernel(plan, place_ref, *refs):
    homes, layers, micros, ranks, room, count = plan
    routes, entering = refs[:homes], refs[homes : 2 * homes]
    sent = refs[2 * homes : 2 * homes + count]
    start_ref, order_ref = refs[2 * homes + count :]
    layer, rank = place_ref[0], place_ref[1]
    tokens = routes[0].shape[1]
    rows = ranks * room
    near = [jnp.maximum(layer - 1, 0), layer, jnp.minimum(layer + 1, layers - 1)]
    ids = [
        [[routes[j][pl.ds(at * micros + m, 1), :] for m in range(micros)] for at in near]
        for j in range(homes)
    ]
    experts = lax.broadcasted_iota(jnp.int32, (ranks, tokens), 0)
    before = (
        lax.broadcasted_iota(jnp.int32, (tokens, tokens), 0)
        < lax.broadcasted_iota(jnp.int32, (tokens, tokens), 1)
    ).astype(f32).astype(bf16)
    flat = [row for home in ids for at in home for row in at]
    marks = jnp.concatenate([(experts == row).astype(f32) for row in flat], axis=0)
    earlier = marks * jnp.dot(marks.astype(bf16), before, preferred_element_type=f32)
    within = [
        jnp.sum(earlier[i * ranks : (i + 1) * ranks], axis=0, keepdims=True).astype(jnp.int32)
        for i in range(len(flat))
    ]

    def one_hot(size, index):
        slots = lax.broadcasted_iota(jnp.int32, (size, tokens), 0)
        return (slots == index).astype(f32).astype(bf16)

    def places(j, at, m):
        row, depth = ids[j][at][m], within[(j * 3 + at) * micros + m]
        if homes == 1:
            index = row * room + depth
            return index, index
        offset = row ^ rank
        far, other = offset >> 1, offset & 1
        target = jnp.where(other == 0, (2 * far + j) * room + depth, -1)
        side = other if j == 0 else 1 - other
        return target, other * rows + (2 * far + side) * room + depth

    for m in range(micros):
        here = [one_hot(rows, places(j, 1, m)[0]) for j in range(homes)]
        for which, at in enumerate((0, 2)):
            total = 0.0
            for j in range(homes):
                there = one_hot(homes * rows, places(j, at, m)[1])
                total += lax.dot_general(here[j], there, LAST, preferred_element_type=f32)
            order_ref[which * micros + m] = total.astype(bf16)
        start = 0.0
        for j in range(homes):
            start += jnp.dot(here[j], entering[j][m], preferred_element_type=f32)
        if m == 0:
            split_rows(sent, start.astype(bf16))
        else:
            start_ref[m - 1] = start.astype(bf16)


def grads_kernel(rows_ref, joined_ref, activated_ref, scaled_ref, in_ref, out_ref):
    total_in, total_out = 0.0, 0.0
    for m in range(rows_ref.shape[0]):
        total_in += lax.dot_general(
            rows_ref[m], joined_ref[m], FIRST, preferred_element_type=f32
        )
        total_out += lax.dot_general(
            activated_ref[m], scaled_ref[m], FIRST, preferred_element_type=f32
        )
    in_ref[...] = total_in.astype(bf16)
    out_ref[...] = total_out.astype(bf16)


def shards(tokens_in, out_grad, routes, router, norm_gain, w_in, w_out):
    layers = lax.axis_size("pipe")
    ranks = lax.axis_size("expert")
    layer = lax.axis_index("pipe")
    rank = lax.axis_index("expert")
    micros, tokens, width = tokens_in.shape
    assert routes.shape[3] == 1 and router.shape[2] == ranks
    assert micros == 2 and layers > 2 and layers % 2 == 0
    capacity = max(2, tokens * 3 // (2 * ranks))
    room = -(-capacity // 8) * 8 if capacity >= 8 else -(-capacity // 4) * 4
    rows = ranks * room
    paired = ranks <= 8 and ranks & (ranks - 1) == 0 and room % 8 == 0
    count = ranks // 2 if paired else 1
    homes = 2 if paired else 1
    size = rows // count
    last = layers - 1
    steps = 2 * last + micros
    own_in, own_out, gain_row = w_in[0, 0], w_out[0, 0], norm_gain
    double, inner = own_in.shape[1], own_out.shape[0]
    column = (
        lax.dynamic_index_in_dim(router[0], rank, 1, keepdims=False).astype(f32).reshape(1, width)
    )
    place = jnp.stack([layer, rank]).astype(jnp.int32)
    piece = jax.ShapeDtypeStruct((size, width), bf16)
    params = pltpu.CompilerParams(vmem_limit_bytes=48 << 20)

    def permuted(block, offset, jump):
        route = []
        for p in range(layers):
            q = p if jump is None else jump(p)
            route += [(p * ranks + i, q * ranks + (i ^ offset)) for i in range(ranks)]
        return lax.ppermute(block, ("pipe", "expert"), route)

    def spread(pieces):
        return lax.all_to_all(
            pieces[0].reshape(ranks, room, width), "expert", split_axis=0, concat_axis=0, tiled=True
        ).reshape(rows, width)

    def to_experts(pieces):
        if not paired:
            return [spread(pieces)]
        arrived = [pieces[0]] + [None] * (count - 1)
        for k in reversed(range(1, count)):
            arrived[k] = permuted(pieces[k], 2 * k, None)
        return arrived

    def to_homes(pieces, jump):
        if not paired:
            return [lax.ppermute(spread(pieces), "pipe", [(p, jump(p)) for p in range(layers)])]
        arrived = [None] * count
        for k in reversed(range(count)):
            arrived[k] = permuted(pieces[k], 2 * k, jump)
        return arrived + [permuted(block, 1, None) for block in arrived]

    entering = jnp.where(layer == 0, tokens_in, out_grad)
    ids = routes.reshape(layers * micros, tokens)
    both_ids, both_entering = [ids], [entering]
    if paired:
        both_ids.append(permuted(ids, 1, None))
        both_entering.append(permuted(entering, 1, None))
    *pieces, start, order = pl.pallas_call(
        functools.partial(prepare_kernel, (homes, layers, micros, ranks, room, count)),
        out_shape=[piece] * count
        + [
            jax.ShapeDtypeStruct((micros - 1, rows, width), bf16),
            jax.ShapeDtypeStruct((2 * micros, rows, homes * rows), bf16),
        ],
        in_specs=[SMEM] + [VMEM] * (2 * homes),
        out_specs=[VMEM] * (count + 2),
        compiler_params=params,
        name="prepare",
    )(place, *both_ids, *both_entering)

    def resort(step, arrived):
        def which(ref):
            forward_micro = step - ref[0]
            backward_micro = jnp.clip(forward_micro - 2 * (last - ref[0]), 0, micros - 1)
            is_forward = (forward_micro >= 0) & (forward_micro < micros)
            return jnp.where(is_forward, forward_micro, micros + backward_micro)

        entry = step < micros
        whole = lambda shape: pl.BlockSpec(shape, lambda i, ref: (0,) * len(shape))
        ins = list(arrived) + ([start[step - 1]] if entry else [])
        return pl.pallas_call(
            functools.partial(resort_kernel, (len(arrived), count, entry, last)),
            out_shape=[piece] * count,
            grid_spec=pltpu.PrefetchScalarGridSpec(
                num_scalar_prefetch=1,
                grid=(1,),
                in_specs=[
                    pl.BlockSpec((1, rows, homes * rows), lambda i, ref: (which(ref), 0, 0))
                ]
                + [whole(value.shape) for value in ins],
                out_specs=[whole((size, width))] * count,
            ),
            compiler_params=params,
            name="resort",
        )(place, order, *ins)

    def forward(arrived):
        out = pl.pallas_call(
            functools.partial(forward_kernel, count),
            out_shape=[piece] * count
            + [
                jax.ShapeDtypeStruct((rows, width), bf16),
                jax.ShapeDtypeStruct((rows, double), f32),
                jax.ShapeDtypeStruct((rows, width), bf16),
            ],
            in_specs=[VMEM] * (4 + count),
            out_specs=[VMEM] * (count + 3),
            compiler_params=params,
            name="forward",
        )(gain_row, column, own_in, own_out, *arrived)
        return out[:count], out[count:]

    kept_sizes = (width, double, inner, width)

    def backward(step, arrived, entered, forwards, kept):
        passes = step + 1 < steps
        plan = (count, layers, micros, step, kept is not None, passes)
        operands = [place, gain_row, column, own_in, own_out, *arrived]
        if step < last + micros:
            operands += entered
        for p in saved_steps(plan):
            operands += forwards[step - 2 * (last - p)]
        specs = [SMEM] + [VMEM] * (len(operands) - 1)
        sent = count if passes else 0
        aliases = {}
        if kept is not None:
            aliases = {len(operands) + i: sent + i for i in range(4)}
            operands += kept
            specs += [ANY] * 4
        out = pl.pallas_call(
            functools.partial(backward_kernel, plan),
            out_shape=[piece] * sent
            + [jax.ShapeDtypeStruct((micros + 1, rows, size), bf16) for size in kept_sizes],
            in_specs=specs,
            out_specs=[VMEM] * sent + [ANY] * 4,
            scratch_shapes=[pltpu.VMEM((rows, size), bf16) for size in kept_sizes]
            + [pltpu.SemaphoreType.DMA((4,))],
            input_output_aliases=aliases,
            compiler_params=params,
            name="backward",
        )(*operands)
        return out[:sent], out[sent:]

    arrivals, forwards = [], []
    kept = None
    for step in range(steps):
        arrived = to_experts(pieces)
        arrivals.append(arrived)
        if step < last + micros:
            pieces, saved = forward(arrived)
            forwards.append(saved)
        if step >= last:
            entered = arrivals[step - last]
            passed, kept = backward(step, arrived, entered, forwards, kept)
            if step == last:
                passed = [jnp.where(layer == last, a, b) for a, b in zip(passed, pieces)]
            pieces = passed
        if step + 1 == steps:
            break
        if step < last:
            jump = lambda p: (p + 1) % layers
        elif step == last:
            jump = lambda p: p ^ 1
        else:
            jump = lambda p: (p - 1) % layers
        pieces = resort(step + 1, to_homes(pieces, jump))

    cuts = 4
    column_block = lambda width: pl.BlockSpec((micros, rows, width), lambda i: (0, 0, i))
    whole_block = lambda width: pl.BlockSpec((micros, rows, width), lambda i: (0, 0, 0))
    grad_in, grad_out = pl.pallas_call(
        grads_kernel,
        grid=(cuts,),
        out_shape=[
            jax.ShapeDtypeStruct((width, double), bf16),
            jax.ShapeDtypeStruct((inner, width), bf16),
        ],
        in_specs=[
            column_block(width // cuts),
            whole_block(double),
            column_block(inner // cuts),
            whole_block(width),
        ],
        out_specs=[
            pl.BlockSpec((width // cuts, double), lambda i: (i, 0)),
            pl.BlockSpec((inner // cuts, width), lambda i: (i, 0)),
        ],
        compiler_params=params,
        name="grads",
    )(*kept)
    return grad_in[None, None], grad_out[None, None]


def solution(mesh):
    placed = (
        P(None, "expert", None),
        P(None, "expert", None),
        P(None, None, "expert", None),
        P("pipe", None, None),
        P("pipe", None),
        P("pipe", "expert", None, None),
        P("pipe", "expert", None, None),
    )
    return jax.shard_map(
        shards,
        mesh=mesh,
        in_specs=placed,
        out_specs=(P("pipe", "expert", None, None), P("pipe", "expert", None, None)),
        check_vma=False,
    )
```

```python
import functools

import jax
import jax.numpy as jnp
from jax import lax
from jax.experimental import pallas as pl
from jax.experimental.pallas import tpu as pltpu
from jax.sharding import PartitionSpec as P

epsilon = 1e-06


f32, bf16 = jnp.float32, jnp.bfloat16
VMEM = pl.BlockSpec(memory_space=pltpu.VMEM)
SMEM = pl.BlockSpec(memory_space=pltpu.SMEM)
ANY = pl.BlockSpec(memory_space=pl.ANY)
LAST = (((1,), (1,)), ((), ()))
FIRST = (((0,), (0,)), ((), ()))


def joined_rows(refs):
    parts = [ref[...] for ref in refs]
    return parts[0] if len(parts) == 1 else jnp.concatenate(parts, axis=0)


def split_rows(refs, value):
    size = refs[0].shape[0]
    for k, ref in enumerate(refs):
        ref[...] = value[k * size : (k + 1) * size]


def normalize(hidden, gain):
    values = hidden.astype(f32)
    inverse = lax.rsqrt(jnp.mean(values * values, axis=-1, keepdims=True) + epsilon)
    scaled = values * inverse
    return (scaled * gain).astype(bf16), scaled, inverse


def gate_of(normed, column):
    return jax.nn.sigmoid(jnp.sum(normed.astype(f32) * column, axis=-1, keepdims=True))


def forward_kernel(count, gain_ref, column_ref, in_ref, out_ref, *refs):
    arrived, sent = refs[:count], refs[count : 2 * count]
    hidden_ref, joined_ref, produced_ref = refs[2 * count :]
    inner = out_ref.shape[0]
    hidden = joined_rows(arrived)
    normed, _, _ = normalize(hidden, gain_ref[...].astype(f32))
    share = gate_of(normed, column_ref[...]).astype(bf16).astype(f32)
    joined = jnp.dot(normed, in_ref[...], preferred_element_type=f32)
    gate_part = joined[:, :inner]
    activated = (gate_part * jax.nn.sigmoid(gate_part) * joined[:, inner:]).astype(bf16)
    produced = jnp.dot(activated, out_ref[...], preferred_element_type=f32).astype(bf16)
    output = (hidden.astype(f32) + share * produced.astype(f32)).astype(bf16)
    split_rows(sent, output)
    hidden_ref[...] = hidden
    joined_ref[...] = joined
    produced_ref[...] = produced


def backward_kernel(plan, place_ref, gain_ref, column_ref, in_ref, out_ref, *refs):
    count, layers, micros, step, aliased, passes = plan
    last = layers - 1
    layer = place_ref[0]
    refs = list(refs)
    take = lambda number: [refs.pop(0) for _ in range(number)]
    arrived = take(count)
    entered = take(count) if step < last + micros else None
    ahead = take(count) if step == last else None
    own = saved_steps(plan)
    saved = [take(3) for _ in own]
    if aliased:
        take(4)
    sent = take(count) if passes else None
    kept = take(4)
    stage = take(4)
    sems = refs.pop(0)
    upstream = joined_rows(arrived)
    if entered is not None:
        upstream = jnp.where(layer == last, joined_rows(entered), upstream)
    upstream_f = upstream.astype(f32)

    def pick(index):
        value = saved[0][index][...]
        for p, group in zip(own[1:], saved[1:]):
            value = jnp.where(layer == p, group[index][...], value)
        return value

    hidden, joined, produced = pick(0), pick(1), pick(2)
    micro = step - (2 * last - layer)
    slot = jnp.where((micro >= 0) & (micro < micros), micro, micros)
    copies = [
        pltpu.make_async_copy(stage[i], kept[i].at[slot], sems.at[i]) for i in range(4)
    ]
    inner = out_ref.shape[1]
    gain, column = gain_ref[...].astype(f32), column_ref[...]
    normed, scaled, inverse = normalize(hidden, gain)
    gate = gate_of(normed, column)
    gate_part, up_part = joined[:, :inner], joined[:, inner:]
    sigmoid_gate = jax.nn.sigmoid(gate_part)
    silu_gate = gate_part * sigmoid_gate
    scaled_grad = (gate.astype(bf16).astype(f32) * upstream_f).astype(bf16)
    stage[0][...] = normed
    stage[2][...] = (silu_gate * up_part).astype(bf16)
    stage[3][...] = scaled_grad
    for i in (0, 2, 3):
        copies[i].start()
    act_grad = jnp.dot(scaled_grad, out_ref[...], preferred_element_type=f32)
    gate_grad = act_grad * up_part * sigmoid_gate * (1.0 + gate_part * (1.0 - sigmoid_gate))
    up_grad = act_grad * silu_gate
    joined_grad = jnp.concatenate([gate_grad, up_grad], axis=-1).astype(bf16)
    stage[1][...] = joined_grad
    copies[1].start()
    if passes:
        rows_grad = jnp.dot(joined_grad, in_ref[...], preferred_element_type=f32).astype(bf16)
        share_grad = jnp.sum(produced.astype(f32) * upstream_f, axis=-1, keepdims=True)
        logit_grad = share_grad.astype(bf16).astype(f32) * gate * (1.0 - gate)
        gained = (rows_grad.astype(f32) + logit_grad * column) * gain
        centred = gained - scaled * jnp.mean(gained * scaled, axis=-1, keepdims=True)
        passed = (upstream_f + inverse * centred).astype(bf16)
        if ahead is not None:
            passed = jnp.where(layer == last, passed, joined_rows(ahead))
        split_rows(sent, passed)
    for copy in copies:
        copy.wait()


def saved_steps(plan):
    _, layers, micros, step, _, _ = plan
    return [p for p in range(layers) if 0 <= step - (2 * (layers - 1) - p) < micros]


def resort_kernel(plan, place_ref, order_ref, *refs):
    arrivals, count, entry, last = plan
    arrived = refs[:arrivals]
    rest = refs[arrivals:]
    sent = rest[-count:]
    value = jnp.dot(order_ref[0], joined_rows(arrived), preferred_element_type=f32).astype(bf16)
    if entry:
        layer = place_ref[0]
        value = jnp.where((layer == 0) | (layer == last), rest[0][...], value)
    split_rows(sent, value)


def prepare_kernel(plan, place_ref, *refs):
    homes, layers, micros, ranks, room, count = plan
    routes, entering = refs[:homes], refs[homes : 2 * homes]
    sent = refs[2 * homes : 2 * homes + count]
    start_ref, order_ref = refs[2 * homes + count :]
    layer, rank = place_ref[0], place_ref[1]
    tokens = routes[0].shape[1]
    rows = ranks * room
    near = [jnp.maximum(layer - 1, 0), layer, jnp.minimum(layer + 1, layers - 1)]
    ids = [
        [[routes[j][pl.ds(at * micros + m, 1), :] for m in range(micros)] for at in near]
        for j in range(homes)
    ]
    experts = lax.broadcasted_iota(jnp.int32, (ranks, tokens), 0)
    before = (
        lax.broadcasted_iota(jnp.int32, (tokens, tokens), 0)
        < lax.broadcasted_iota(jnp.int32, (tokens, tokens), 1)
    ).astype(f32).astype(bf16)
    flat = [row for home in ids for at in home for row in at]
    marks = jnp.concatenate([(experts == row).astype(f32) for row in flat], axis=0)
    earlier = marks * jnp.dot(marks.astype(bf16), before, preferred_element_type=f32)
    within = [
        jnp.sum(earlier[i * ranks : (i + 1) * ranks], axis=0, keepdims=True).astype(jnp.int32)
        for i in range(len(flat))
    ]

    def one_hot(size, index):
        slots = lax.broadcasted_iota(jnp.int32, (size, tokens), 0)
        return (slots == index).astype(f32).astype(bf16)

    def places(j, at, m):
        row, depth = ids[j][at][m], within[(j * 3 + at) * micros + m]
        if homes == 1:
            index = row * room + depth
            return index, index
        offset = row ^ rank
        far, other = offset >> 1, offset & 1
        target = jnp.where(other == 0, (2 * far + j) * room + depth, -1)
        side = other if j == 0 else 1 - other
        return target, other * rows + (2 * far + side) * room + depth

    for m in range(micros):
        here = [one_hot(rows, places(j, 1, m)[0]) for j in range(homes)]
        for which, at in enumerate((0, 2)):
            total = 0.0
            for j in range(homes):
                there = one_hot(homes * rows, places(j, at, m)[1])
                total += lax.dot_general(here[j], there, LAST, preferred_element_type=f32)
            order_ref[which * micros + m] = total.astype(bf16)
        start = 0.0
        for j in range(homes):
            start += jnp.dot(here[j], entering[j][m], preferred_element_type=f32)
        if m == 0:
            split_rows(sent, start.astype(bf16))
        else:
            start_ref[m - 1] = start.astype(bf16)


def transpose_kernel(in_ref, out_ref, in_turned, out_turned):
    in_turned[...] = in_ref[...].T
    out_turned[...] = out_ref[...].T


def grads_kernel(parts, *refs):
    in_ref, out_ref = refs[4 * parts :]
    total_in, total_out = 0.0, 0.0
    for part in range(parts):
        rows_ref, joined_ref, activated_ref, scaled_ref = refs[4 * part : 4 * part + 4]
        for m in range(rows_ref.shape[0]):
            total_in += lax.dot_general(
                rows_ref[m], joined_ref[m], FIRST, preferred_element_type=f32
            )
            total_out += lax.dot_general(
                activated_ref[m], scaled_ref[m], FIRST, preferred_element_type=f32
            )
    in_ref[...] = total_in.astype(bf16)
    out_ref[...] = total_out.astype(bf16)


def shards(tokens_in, out_grad, routes, router, norm_gain, w_in, w_out):
    layers = lax.axis_size("pipe")
    ranks = lax.axis_size("expert")
    layer = lax.axis_index("pipe")
    rank = lax.axis_index("expert")
    micros, tokens, width = tokens_in.shape
    assert routes.shape[3] == 1 and router.shape[2] == ranks
    assert micros == 2 and layers > 2 and layers % 2 == 0
    capacity = max(2, tokens * 3 // (2 * ranks))
    room = -(-capacity // 8) * 8 if capacity >= 8 else -(-capacity // 4) * 4
    rows = ranks * room
    paired = ranks <= 8 and ranks & (ranks - 1) == 0 and room % 8 == 0
    count = ranks // 2 if paired else 1
    parts = [[0,3],[1,2]] if count == 4 else [list(range(count))]
    homes = 2 if paired else 1
    size = rows // count
    last = layers - 1
    steps = 2 * last + micros
    own_in, own_out, gain_row = w_in[0, 0], w_out[0, 0], norm_gain
    double, inner = own_in.shape[1], own_out.shape[0]
    column = (
        lax.dynamic_index_in_dim(router[0], rank, 1, keepdims=False).astype(f32).reshape(1, width)
    )
    place = jnp.stack([layer, rank]).astype(jnp.int32)
    piece = jax.ShapeDtypeStruct((size, width), bf16)
    params = pltpu.CompilerParams(vmem_limit_bytes=16 << 20)

    def permuted(block, offset, jump):
        route = []
        for p in range(layers):
            q = p if jump is None else jump(p)
            route += [(p * ranks + i, q * ranks + (i ^ offset)) for i in range(ranks)]
        return lax.ppermute(block, ("pipe", "expert"), route)

    def spread(pieces):
        return lax.all_to_all(
            pieces[0].reshape(ranks, room, width), "expert", split_axis=0, concat_axis=0, tiled=True
        ).reshape(rows, width)

    def to_experts(pieces):
        if not paired:
            return [spread(pieces)]
        arrived = [pieces[0]] + [None] * (count - 1)
        for k in sorted(range(1, count), key=lambda k: (k % 2, -k)):
            arrived[k] = permuted(pieces[k], 2 * k, None)
        return arrived

    def to_homes(pieces, jump):
        if not paired:
            return [lax.ppermute(spread(pieces), "pipe", [(p, jump(p)) for p in range(layers)])]
        arrived, swapped = [None] * count, [None] * count
        for part in parts:
            for k in reversed(part):
                arrived[k] = permuted(pieces[k], 2 * k, jump)
                swapped[k] = permuted(arrived[k], 1, None)
        return arrived + swapped

    entering = jnp.where(layer == 0, tokens_in, out_grad)
    ids = routes.reshape(layers * micros, tokens)
    both_ids, both_entering = [ids], [entering]
    if paired:
        both_ids.append(permuted(ids, 1, None))
        both_entering.append(permuted(entering, 1, None))
    *pieces, start, order = pl.pallas_call(
        functools.partial(prepare_kernel, (homes, layers, micros, ranks, room, count)),
        out_shape=[piece] * count
        + [
            jax.ShapeDtypeStruct((micros - 1, rows, width), bf16),
            jax.ShapeDtypeStruct((2 * micros, rows, homes * rows), bf16),
        ],
        in_specs=[SMEM] + [VMEM] * (2 * homes),
        out_specs=[VMEM] * (count + 2),
        compiler_params=params,
        name="prepare",
    )(place, *both_ids, *both_entering)

    def resort(step, arrived):
        def which(ref):
            forward_micro = step - ref[0]
            backward_micro = jnp.clip(forward_micro - 2 * (last - ref[0]), 0, micros - 1)
            is_forward = (forward_micro >= 0) & (forward_micro < micros)
            return jnp.where(is_forward, forward_micro, micros + backward_micro)

        entry = step < micros
        whole = lambda shape: pl.BlockSpec(shape, lambda i, ref: (0,) * len(shape))
        ins = list(arrived) + ([start[step - 1]] if entry else [])
        return pl.pallas_call(
            functools.partial(resort_kernel, (len(arrived), count, entry, last)),
            out_shape=[piece] * count,
            grid_spec=pltpu.PrefetchScalarGridSpec(
                num_scalar_prefetch=1,
                grid=(1,),
                in_specs=[
                    pl.BlockSpec((1, rows, homes * rows), lambda i, ref: (which(ref), 0, 0))
                ]
                + [whole(value.shape) for value in ins],
                out_specs=[whole((size, width))] * count,
            ),
            compiler_params=params,
            name="resort",
        )(place, order, *ins)

    def forward(arrived):
        many = len(arrived)
        out = pl.pallas_call(
            functools.partial(forward_kernel, many),
            out_shape=[piece] * many
            + [
                jax.ShapeDtypeStruct((many * size, width), bf16),
                jax.ShapeDtypeStruct((many * size, double), f32),
                jax.ShapeDtypeStruct((many * size, width), bf16),
            ],
            in_specs=[VMEM] * (4 + many),
            out_specs=[VMEM] * (many + 3),
            compiler_params=params,
            name="forward",
        )(gain_row, column, own_in, own_out, *arrived)
        return out[:many], out[many:]

    kept_sizes = (width, double, inner, width)
    turned_in, turned_out = pl.pallas_call(
        transpose_kernel,
        out_shape=[
            jax.ShapeDtypeStruct((double, width), bf16),
            jax.ShapeDtypeStruct((width, inner), bf16),
        ],
        in_specs=[VMEM] * 2,
        out_specs=[VMEM] * 2,
        compiler_params=params,
        name="turn",
    )(own_in, own_out)

    def backward(step, arrived, entered, ahead, saved, kept):
        passes = step + 1 < steps
        many = len(arrived)
        plan = (many, layers, micros, step, kept is not None, passes)
        operands = [place, gain_row, column, turned_in, turned_out, *arrived]
        if step < last + micros:
            operands += entered
        if step == last:
            operands += ahead
        for p in saved_steps(plan):
            operands += saved[step - 2 * (last - p)]
        specs = [SMEM] + [VMEM] * (len(operands) - 1)
        sent = many if passes else 0
        aliases = {}
        if kept is not None:
            aliases = {len(operands) + i: sent + i for i in range(4)}
            operands += kept
            specs += [ANY] * 4
        held = [(many * size, length) for length in kept_sizes]
        out = pl.pallas_call(
            functools.partial(backward_kernel, plan),
            out_shape=[piece] * sent
            + [jax.ShapeDtypeStruct((micros + 1, *shape), bf16) for shape in held],
            in_specs=specs,
            out_specs=[VMEM] * sent + [ANY] * 4,
            scratch_shapes=[pltpu.VMEM(shape, bf16) for shape in held]
            + [pltpu.SemaphoreType.DMA((4,))],
            input_output_aliases=aliases,
            compiler_params=params,
            name="backward",
        )(*operands)
        return out[:sent], out[sent:]

    arrivals = []
    forwards = [[] for _ in parts]
    kept = [None for _ in parts]
    for step in range(steps):
        arrived = to_experts(pieces)
        arrivals.append(arrived)
        pieces = [None] * count
        for index, part in enumerate(parts):
            here = [arrived[k] for k in part]
            passed = None
            if step < last + micros:
                passed, saved = forward(here)
                forwards[index].append(saved)
            if step >= last:
                entered = [arrivals[step - last][k] for k in part]
                passed, kept[index] = backward(
                    step, here, entered, passed, forwards[index], kept[index]
                )
            for k, value in zip(part, passed):
                pieces[k] = value
        if step + 1 == steps:
            break
        if step < last:
            jump = lambda p: (p + 1) % layers
        elif step == last:
            jump = lambda p: p ^ 1
        else:
            jump = lambda p: (p - 1) % layers
        pieces = resort(step + 1, to_homes(pieces, jump))

    cuts = 4
    specs = []
    for part in parts:
        depth = len(part) * size
        column_block = lambda length: pl.BlockSpec((micros, depth, length), lambda i: (0, 0, i))
        whole_block = lambda length: pl.BlockSpec((micros, depth, length), lambda i: (0, 0, 0))
        specs += [
            column_block(width // cuts),
            whole_block(double),
            column_block(inner // cuts),
            whole_block(width),
        ]
    grad_in, grad_out = pl.pallas_call(
        functools.partial(grads_kernel, len(parts)),
        grid=(cuts,),
        out_shape=[
            jax.ShapeDtypeStruct((width, double), bf16),
            jax.ShapeDtypeStruct((inner, width), bf16),
        ],
        in_specs=specs,
        out_specs=[
            pl.BlockSpec((width // cuts, double), lambda i: (i, 0)),
            pl.BlockSpec((inner // cuts, width), lambda i: (i, 0)),
        ],
        compiler_params=params,
        name="grads",
    )(*[buffer for group in kept for buffer in group])
    return grad_in[None, None], grad_out[None, None]


def solution(mesh):
    placed = (
        P(None, "expert", None),
        P(None, "expert", None),
        P(None, None, "expert", None),
        P("pipe", None, None),
        P("pipe", None),
        P("pipe", "expert", None, None),
        P("pipe", "expert", None, None),
    )
    return jax.shard_map(
        shards,
        mesh=mesh,
        in_specs=placed,
        out_specs=(P("pipe", "expert", None, None), P("pipe", "expert", None, None)),
        check_vma=False,
    )
```

```python
import functools

import jax
import jax.numpy as jnp
from jax import lax
from jax.experimental import pallas as pl
from jax.experimental.pallas import tpu as pltpu
from jax.sharding import PartitionSpec as P

epsilon = 1e-06


f32, bf16 = jnp.float32, jnp.bfloat16
VMEM = pl.BlockSpec(memory_space=pltpu.VMEM)
SMEM = pl.BlockSpec(memory_space=pltpu.SMEM)
ANY = pl.BlockSpec(memory_space=pl.ANY)
LAST = (((1,), (1,)), ((), ()))
FIRST = (((0,), (0,)), ((), ()))
LANES = 128


def unpacked(ref, width):
    value = ref[...]
    size = value.shape[0]
    if value.shape[1] == width:
        return value
    real = size - 2
    spare = value[real:].astype(f32)
    blocks = [spare[:, i * LANES : (i + 1) * LANES] for i in range(real // 2)]
    tail = jnp.concatenate(blocks + [jnp.zeros((2, LANES), f32)], axis=0).astype(bf16)
    held = lax.broadcasted_iota(jnp.int32, value.shape, 0) < real
    return jnp.concatenate([jnp.where(held, value, jnp.zeros_like(value)), tail], axis=1)


def packed(value, short):
    if value.shape[1] == short:
        return value
    real = value.shape[0] - 2
    tail = value[:, short:].astype(f32)
    spare = jnp.concatenate([tail[2 * i : 2 * i + 2] for i in range(real // 2)], axis=1)
    last = value[-16:, :short].astype(f32)
    last = jnp.concatenate([last[:14], spare], axis=0).astype(bf16)
    return jnp.concatenate([value[:-16, :short], last], axis=0)


def joined_rows(refs, width):
    parts = [unpacked(ref, width) for ref in refs]
    return parts[0] if len(parts) == 1 else jnp.concatenate(parts, axis=0)


def split_rows(refs, value, keep=None, others=None):
    size, short = refs[0].shape
    for k, ref in enumerate(refs):
        block = packed(value[k * size : (k + 1) * size], short)
        if others is not None:
            block = jnp.where(keep, block, others[k][...])
        ref[...] = block


def normalize(hidden, gain):
    values = hidden.astype(f32)
    inverse = lax.rsqrt(jnp.mean(values * values, axis=-1, keepdims=True) + epsilon)
    scaled = values * inverse
    return (scaled * gain).astype(bf16), scaled, inverse


def gate_of(normed, column):
    return jax.nn.sigmoid(jnp.sum(normed.astype(f32) * column, axis=-1, keepdims=True))


def forward_kernel(count, gain_ref, column_ref, in_ref, out_ref, *refs):
    arrived, sent = refs[:count], refs[count : 2 * count]
    hidden_ref, joined_ref, produced_ref = refs[2 * count :]
    inner = out_ref.shape[0]
    hidden = joined_rows(arrived, in_ref.shape[0])
    normed, _, _ = normalize(hidden, gain_ref[...].astype(f32))
    share = gate_of(normed, column_ref[...]).astype(bf16).astype(f32)
    joined = jnp.dot(normed, in_ref[...], preferred_element_type=f32)
    gate_part = joined[:, :inner]
    activated = (gate_part * jax.nn.sigmoid(gate_part) * joined[:, inner:]).astype(bf16)
    produced = jnp.dot(activated, out_ref[...], preferred_element_type=f32).astype(bf16)
    output = (hidden.astype(f32) + share * produced.astype(f32)).astype(bf16)
    split_rows(sent, output)
    hidden_ref[...] = hidden
    joined_ref[...] = joined
    produced_ref[...] = produced


def backward_kernel(plan, place_ref, gain_ref, column_ref, in_ref, out_ref, *refs):
    count, layers, micros, sets, enters, first, aliased, passes = plan
    last = layers - 1
    layer, step = place_ref[0], place_ref[2]
    refs = list(refs)
    take = lambda number: [refs.pop(0) for _ in range(number)]
    arrived = take(count)
    entered = take(count) if enters else None
    ahead = take(count) if first else None
    saved = [take(3) for _ in range(sets)]
    if aliased:
        take(4)
    sent = take(count) if passes else None
    kept = take(4)
    stage = take(4)
    sems = refs.pop(0)
    width = out_ref.shape[0]
    upstream = joined_rows(arrived, width)
    if entered is not None:
        upstream = jnp.where(layer == last, joined_rows(entered, width), upstream)
    upstream_f = upstream.astype(f32)
    micro = step - (2 * last - layer)

    def pick(index):
        value = saved[0][index][...]
        for group in saved[1:]:
            value = jnp.where(micro == 1, group[index][...], value)
        return value

    hidden, joined, produced = pick(0), pick(1), pick(2)
    slot = jnp.where((micro >= 0) & (micro < micros), micro, micros)
    copies = [
        pltpu.make_async_copy(stage[i], kept[i].at[slot], sems.at[i]) for i in range(4)
    ]
    inner = out_ref.shape[1]
    gain, column = gain_ref[...].astype(f32), column_ref[...]
    normed, scaled, inverse = normalize(hidden, gain)
    gate = gate_of(normed, column)
    gate_part, up_part = joined[:, :inner], joined[:, inner:]
    sigmoid_gate = jax.nn.sigmoid(gate_part)
    silu_gate = gate_part * sigmoid_gate
    scaled_grad = (gate.astype(bf16).astype(f32) * upstream_f).astype(bf16)
    stage[0][...] = normed
    stage[2][...] = (silu_gate * up_part).astype(bf16)
    stage[3][...] = scaled_grad
    for i in (0, 2, 3):
        copies[i].start()
    act_grad = jnp.dot(scaled_grad, out_ref[...], preferred_element_type=f32)
    gate_grad = act_grad * up_part * sigmoid_gate * (1.0 + gate_part * (1.0 - sigmoid_gate))
    up_grad = act_grad * silu_gate
    joined_grad = jnp.concatenate([gate_grad, up_grad], axis=-1).astype(bf16)
    stage[1][...] = joined_grad
    copies[1].start()
    if passes:
        rows_grad = jnp.dot(joined_grad, in_ref[...], preferred_element_type=f32).astype(bf16)
        share_grad = jnp.sum(produced.astype(f32) * upstream_f, axis=-1, keepdims=True)
        logit_grad = share_grad.astype(bf16).astype(f32) * gate * (1.0 - gate)
        gained = (rows_grad.astype(f32) + logit_grad * column) * gain
        centred = gained - scaled * jnp.mean(gained * scaled, axis=-1, keepdims=True)
        passed = (upstream_f + inverse * centred).astype(bf16)
        split_rows(sent, passed, layer == last, ahead)
    for copy in copies:
        copy.wait()


def resort_kernel(plan, place_ref, order_ref, *refs):
    arrivals, count, width, entry, last = plan
    arrived = refs[:arrivals]
    rest = refs[arrivals:]
    sent = rest[-count:]
    value = jnp.dot(
        order_ref[0], joined_rows(arrived, width), preferred_element_type=f32
    ).astype(bf16)
    if entry:
        layer = place_ref[0]
        value = jnp.where((layer == 0) | (layer == last), rest[0][...], value)
    split_rows(sent, value)


def prepare_kernel(plan, place_ref, *refs):
    homes, layers, micros, ranks, room, size, count = plan
    routes, entering = refs[:homes], refs[homes : 2 * homes]
    sent = refs[2 * homes : 2 * homes + count]
    start_ref, order_ref = refs[2 * homes + count :]
    layer, rank = place_ref[0], place_ref[1]
    tokens = routes[0].shape[1]
    rows = size * count
    near = [jnp.maximum(layer - 1, 0), layer, jnp.minimum(layer + 1, layers - 1)]
    ids = [
        [[routes[j][pl.ds(at * micros + m, 1), :] for m in range(micros)] for at in near]
        for j in range(homes)
    ]
    experts = lax.broadcasted_iota(jnp.int32, (ranks, tokens), 0)
    before = (
        lax.broadcasted_iota(jnp.int32, (tokens, tokens), 0)
        < lax.broadcasted_iota(jnp.int32, (tokens, tokens), 1)
    ).astype(f32).astype(bf16)
    flat = [row for home in ids for at in home for row in at]
    marks = jnp.concatenate([(experts == row).astype(f32) for row in flat], axis=0)
    earlier = marks * jnp.dot(marks.astype(bf16), before, preferred_element_type=f32)
    within = [
        jnp.sum(earlier[i * ranks : (i + 1) * ranks], axis=0, keepdims=True).astype(jnp.int32)
        for i in range(len(flat))
    ]

    def one_hot(size, index):
        slots = lax.broadcasted_iota(jnp.int32, (size, tokens), 0)
        return (slots == index).astype(f32).astype(bf16)

    def places(j, at, m):
        row, depth = ids[j][at][m], within[(j * 3 + at) * micros + m]
        if homes == 1:
            index = row * room + depth
            return index, index
        offset = row ^ rank
        far, other = offset >> 1, offset & 1
        target = jnp.where(other == 0, far * size + j * room + depth, -1)
        side = other if j == 0 else 1 - other
        return target, other * rows + far * size + side * room + depth

    for m in range(micros):
        here = [one_hot(rows, places(j, 1, m)[0]) for j in range(homes)]
        for which, at in enumerate((0, 2)):
            total = 0.0
            for j in range(homes):
                there = one_hot(homes * rows, places(j, at, m)[1])
                total += lax.dot_general(here[j], there, LAST, preferred_element_type=f32)
            order_ref[which * micros + m] = total.astype(bf16)
        start = 0.0
        for j in range(homes):
            start += jnp.dot(here[j], entering[j][m], preferred_element_type=f32)
        if m == 0:
            split_rows(sent, start.astype(bf16))
        else:
            start_ref[m - 1] = start.astype(bf16)


def transpose_kernel(in_ref, out_ref, in_turned, out_turned):
    in_turned[...] = in_ref[...].T
    out_turned[...] = out_ref[...].T


def grads_kernel(parts, *refs):
    in_ref, out_ref = refs[4 * parts :]

    def gathered(which):
        groups = [refs[4 * part + which] for part in range(parts)]
        return jnp.concatenate([g[m] for g in groups for m in range(g.shape[0])], axis=0)

    in_ref[...] = lax.dot_general(
        gathered(0), gathered(1), FIRST, preferred_element_type=f32
    ).astype(bf16)
    out_ref[...] = lax.dot_general(
        gathered(2), gathered(3), FIRST, preferred_element_type=f32
    ).astype(bf16)


def shards(tokens_in, out_grad, routes, router, norm_gain, w_in, w_out):
    layers = lax.axis_size("pipe")
    ranks = lax.axis_size("expert")
    layer = lax.axis_index("pipe")
    rank = lax.axis_index("expert")
    micros, tokens, width = tokens_in.shape
    assert routes.shape[3] == 1 and router.shape[2] == ranks
    assert micros == 2 and layers > 2 and layers % 2 == 0
    capacity = max(2, tokens * 3 // (2 * ranks))
    paired = ranks <= 8 and ranks & (ranks - 1) == 0 and capacity >= 8
    count = ranks // 2 if paired else 1
    homes = 2 if paired else 1
    if paired:
        room = capacity
        size = -(-2 * room // 16) * 16
    else:
        room = -(-capacity // 4) * 4
        size = ranks * room
    rows = size * count
    tight = paired and size == 2 * room + 2 and width == LANES * (room + 1)
    short = width - LANES if tight else width
    parts = [[0, 3], [1, 2]] if count == 4 else [list(range(count))]
    last = layers - 1
    steps = 2 * last + micros
    own_in, own_out, gain_row = w_in[0, 0], w_out[0, 0], norm_gain
    double, inner = own_in.shape[1], own_out.shape[0]
    column = (
        lax.dynamic_index_in_dim(router[0], rank, 1, keepdims=False).astype(f32).reshape(1, width)
    )
    places = [
        jnp.stack([layer, rank, jnp.int32(step)]).astype(jnp.int32) for step in range(steps)
    ]
    piece = jax.ShapeDtypeStruct((size, short), bf16)
    params = pltpu.CompilerParams(vmem_limit_bytes=16 << 20)

    def permuted(block, offset, jump):
        route = []
        for p in range(layers):
            q = p if jump is None else jump(p)
            route += [(p * ranks + i, q * ranks + (i ^ offset)) for i in range(ranks)]
        return lax.ppermute(block, ("pipe", "expert"), route)

    def spread(pieces):
        return lax.all_to_all(
            pieces[0].reshape(ranks, room, width), "expert", split_axis=0, concat_axis=0, tiled=True
        ).reshape(rows, width)

    def to_experts(pieces):
        if not paired:
            return [spread(pieces)]
        arrived = [pieces[0]] + [None] * (count - 1)
        for k in sorted(range(1, count), key=lambda k: (k % 2, -k)):
            arrived[k] = permuted(pieces[k], 2 * k, None)
        return arrived

    def to_homes(pieces, jump):
        if not paired:
            return [lax.ppermute(spread(pieces), "pipe", [(p, jump(p)) for p in range(layers)])]
        arrived, swapped = [None] * count, [None] * count
        for part in parts:
            for k in reversed(part):
                arrived[k] = permuted(pieces[k], 2 * k, jump)
                swapped[k] = permuted(arrived[k], 1, None)
        return arrived + swapped

    entering = jnp.where(layer == 0, tokens_in, out_grad)
    ids = routes.reshape(layers * micros, tokens)
    both_ids, both_entering = [ids], [entering]
    if paired:
        both_ids.append(permuted(ids, 1, None))
        both_entering.append(permuted(entering, 1, None))
    *pieces, start, order = pl.pallas_call(
        functools.partial(prepare_kernel, (homes, layers, micros, ranks, room, size, count)),
        out_shape=[piece] * count
        + [
            jax.ShapeDtypeStruct((micros - 1, rows, width), bf16),
            jax.ShapeDtypeStruct((2 * micros, rows, homes * rows), bf16),
        ],
        in_specs=[SMEM] + [VMEM] * (2 * homes),
        out_specs=[VMEM] * (count + 2),
        compiler_params=params,
        name="prepare",
    )(places[0], *both_ids, *both_entering)

    def resort(step, arrived):
        def which(ref):
            forward_micro = ref[2] - ref[0]
            backward_micro = jnp.clip(forward_micro - 2 * (last - ref[0]), 0, micros - 1)
            is_forward = (forward_micro >= 0) & (forward_micro < micros)
            return jnp.where(is_forward, forward_micro, micros + backward_micro)

        entry = step < micros
        whole = lambda shape: pl.BlockSpec(shape, lambda i, ref: (0,) * len(shape))
        ins = list(arrived) + ([start[step - 1]] if entry else [])
        return pl.pallas_call(
            functools.partial(resort_kernel, (len(arrived), count, width, entry, last)),
            out_shape=[piece] * count,
            grid_spec=pltpu.PrefetchScalarGridSpec(
                num_scalar_prefetch=1,
                grid=(1,),
                in_specs=[
                    pl.BlockSpec((1, rows, homes * rows), lambda i, ref: (which(ref), 0, 0))
                ]
                + [whole(value.shape) for value in ins],
                out_specs=[whole((size, short))] * count,
            ),
            compiler_params=params,
            name="resort",
        )(places[step], order, *ins)

    def forward(arrived):
        many = len(arrived)
        out = pl.pallas_call(
            functools.partial(forward_kernel, many),
            out_shape=[piece] * many
            + [
                jax.ShapeDtypeStruct((many * size, width), bf16),
                jax.ShapeDtypeStruct((many * size, double), f32),
                jax.ShapeDtypeStruct((many * size, width), bf16),
            ],
            in_specs=[VMEM] * (4 + many),
            out_specs=[VMEM] * (many + 3),
            compiler_params=params,
            name="forward",
        )(gain_row, column, own_in, own_out, *arrived)
        return out[:many], out[many:]

    kept_sizes = (width, double, inner, width)
    bands = 8
    turned_in, turned_out = pl.pallas_call(
        transpose_kernel,
        grid=(bands,),
        out_shape=[
            jax.ShapeDtypeStruct((double, width), bf16),
            jax.ShapeDtypeStruct((width, inner), bf16),
        ],
        in_specs=[
            pl.BlockSpec((width // bands, double), lambda i: (i, 0)),
            pl.BlockSpec((inner, width // bands), lambda i: (0, i)),
        ],
        out_specs=[
            pl.BlockSpec((double, width // bands), lambda i: (0, i)),
            pl.BlockSpec((width // bands, inner), lambda i: (i, 0)),
        ],
        compiler_params=params,
        name="turn",
    )(own_in, own_out)

    def backward(step, arrived, entered, ahead, saved, kept):
        passes = step + 1 < steps
        many = len(arrived)
        sources = [
            saved[step - 2 * (last - p)]
            for p in range(layers)
            if 0 <= step - (2 * last - p) < micros
        ]
        plan = (
            many,
            layers,
            micros,
            len(sources),
            entered is not None,
            step == last,
            kept is not None,
            passes,
        )
        operands = [places[step], gain_row, column, turned_in, turned_out, *arrived]
        if entered is not None:
            operands += entered
        if step == last:
            operands += ahead
        for group in sources:
            operands += group
        specs = [SMEM] + [VMEM] * (len(operands) - 1)
        sent = many if passes else 0
        aliases = {}
        if kept is not None:
            aliases = {len(operands) + i: sent + i for i in range(4)}
            operands += kept
            specs += [ANY] * 4
        held = [(many * size, length) for length in kept_sizes]
        out = pl.pallas_call(
            functools.partial(backward_kernel, plan),
            out_shape=[piece] * sent
            + [jax.ShapeDtypeStruct((micros + 1, *shape), bf16) for shape in held],
            in_specs=specs,
            out_specs=[VMEM] * sent + [ANY] * 4,
            scratch_shapes=[pltpu.VMEM(shape, bf16) for shape in held]
            + [pltpu.SemaphoreType.DMA((4,))],
            input_output_aliases=aliases,
            compiler_params=params,
            name="backward",
        )(*operands)
        return out[:sent], out[sent:]

    arrivals = []
    forwards = [[] for _ in parts]
    kept = [None for _ in parts]
    for step in range(steps):
        arrived = to_experts(pieces)
        arrivals.append(arrived)
        pieces = [None] * count
        for index, part in enumerate(parts):
            here = [arrived[k] for k in part]
            passed = None
            if step < last + micros:
                passed, saved = forward(here)
                forwards[index].append(saved)
            if step >= last:
                entered = None
                if step < last + micros:
                    entered = [arrivals[step - last][k] for k in part]
                passed, kept[index] = backward(
                    step, here, entered, passed, forwards[index], kept[index]
                )
            for k, value in zip(part, passed):
                pieces[k] = value
        if step + 1 == steps:
            break
        if step < last:
            jump = lambda p: (p + 1) % layers
        elif step == last:
            jump = lambda p: p ^ 1
        else:
            jump = lambda p: (p - 1) % layers
        pieces = resort(step + 1, to_homes(pieces, jump))

    cuts = 4
    specs = []
    for part in parts:
        depth = len(part) * size
        column_block = lambda length: pl.BlockSpec((micros, depth, length), lambda i: (0, 0, i))
        whole_block = lambda length: pl.BlockSpec((micros, depth, length), lambda i: (0, 0, 0))
        specs += [
            column_block(width // cuts),
            whole_block(double),
            column_block(inner // cuts),
            whole_block(width),
        ]
    grad_in, grad_out = pl.pallas_call(
        functools.partial(grads_kernel, len(parts)),
        grid=(cuts,),
        out_shape=[
            jax.ShapeDtypeStruct((width, double), bf16),
            jax.ShapeDtypeStruct((inner, width), bf16),
        ],
        in_specs=specs,
        out_specs=[
            pl.BlockSpec((width // cuts, double), lambda i: (i, 0)),
            pl.BlockSpec((inner // cuts, width), lambda i: (i, 0)),
        ],
        compiler_params=params,
        name="grads",
    )(*[buffer for group in kept for buffer in group])
    return grad_in[None, None], grad_out[None, None]


def solution(mesh):
    placed = (
        P(None, "expert", None),
        P(None, "expert", None),
        P(None, None, "expert", None),
        P("pipe", None, None),
        P("pipe", None),
        P("pipe", "expert", None, None),
        P("pipe", "expert", None, None),
    )
    return jax.shard_map(
        shards,
        mesh=mesh,
        in_specs=placed,
        out_specs=(P("pipe", "expert", None, None), P("pipe", "expert", None, None)),
        check_vma=False,
    )
```

```python
import functools

import jax
import jax.numpy as jnp
from jax import lax
from jax.experimental import pallas as pl
from jax.experimental.pallas import tpu as pltpu
from jax.sharding import PartitionSpec as P


epsilon = 1e-06


f32, bf16 = jnp.float32, jnp.bfloat16
VMEM = pl.BlockSpec(memory_space=pltpu.VMEM)
SMEM = pl.BlockSpec(memory_space=pltpu.SMEM)
ANY = pl.BlockSpec(memory_space=pl.ANY)
LAST = (((1,), (1,)), ((), ()))
FIRST = (((0,), (0,)), ((), ()))
LANES = 128
WIDEST = 8


def unpacked(ref, width):
    value = ref[...]
    size = value.shape[0]
    if value.shape[1] == width:
        return value
    real = size - 2
    spare = value[real:].astype(f32)
    blocks = [spare[:, i * LANES : (i + 1) * LANES] for i in range(real // 2)]
    tail = jnp.concatenate(blocks + [jnp.zeros((2, LANES), f32)], axis=0).astype(bf16)
    held = lax.broadcasted_iota(jnp.int32, value.shape, 0) < real
    return jnp.concatenate([jnp.where(held, value, jnp.zeros_like(value)), tail], axis=1)


def packed(value, short):
    if value.shape[1] == short:
        return value
    real = value.shape[0] - 2
    tail = value[:, short:].astype(f32)
    spare = jnp.concatenate([tail[2 * i : 2 * i + 2] for i in range(real // 2)], axis=1)
    last = value[-16:, :short].astype(f32)
    last = jnp.concatenate([last[:14], spare], axis=0).astype(bf16)
    return jnp.concatenate([value[:-16, :short], last], axis=0)


def joined_rows(refs, width):
    parts = [unpacked(ref, width) for ref in refs]
    return parts[0] if len(parts) == 1 else jnp.concatenate(parts, axis=0)


def split_rows(refs, value, keep=None, others=None):
    size, short = refs[0].shape
    for k, ref in enumerate(refs):
        block = packed(value[k * size : (k + 1) * size], short)
        if others is not None:
            block = jnp.where(keep, block, others[k][...])
        ref[...] = block


def normalize(hidden, gain):
    values = hidden.astype(f32)
    inverse = lax.rsqrt(jnp.mean(values * values, axis=-1, keepdims=True) + epsilon)
    scaled = values * inverse
    return (scaled * gain).astype(bf16), scaled, inverse


def gate_of(normed, column):
    return jax.nn.sigmoid(jnp.sum(normed.astype(f32) * column, axis=-1, keepdims=True))


def forward_kernel(count, chained, gain_ref, column_ref, in_ref, out_ref, *refs):
    arrived, refs = refs[:count], refs[count + chained :]
    sent, refs = refs[:count], refs[count:]
    hidden_ref, joined_ref, produced_ref = refs
    inner = out_ref.shape[0]
    hidden = joined_rows(arrived, in_ref.shape[0])
    normed, _, _ = normalize(hidden, gain_ref[...].astype(f32))
    share = gate_of(normed, column_ref[...]).astype(bf16).astype(f32)
    joined = jnp.dot(normed, in_ref[...], preferred_element_type=f32)
    gate_part = joined[:, :inner]
    activated = (gate_part * jax.nn.sigmoid(gate_part) * joined[:, inner:]).astype(bf16)
    produced = jnp.dot(activated, out_ref[...], preferred_element_type=f32).astype(bf16)
    output = (hidden.astype(f32) + share * produced.astype(f32)).astype(bf16)
    split_rows(sent, output)
    hidden_ref[...] = hidden
    joined_ref[...] = joined
    produced_ref[...] = produced


def backward_kernel(plan, place_ref, gain_ref, column_ref, in_ref, out_ref, *refs):
    count, layers, micros, sets, enters, first, chained, aliased, passes = plan
    last = layers - 1
    layer, step = place_ref[0], place_ref[2]
    refs = list(refs)
    take = lambda number: [refs.pop(0) for _ in range(number)]
    arrived = take(count)
    entered = take(count) if enters else None
    ahead = take(count) if first else None
    saved = [take(3) for _ in range(sets)]
    take(chained)
    if aliased:
        take(4)
    sent = take(count) if passes else None
    kept = take(4)
    stage = take(4)
    sems = refs.pop(0)
    width = out_ref.shape[0]
    upstream = joined_rows(arrived, width)
    if entered is not None:
        upstream = jnp.where(layer == last, joined_rows(entered, width), upstream)
    upstream_f = upstream.astype(f32)
    micro = step - (2 * last - layer)

    def pick(index):
        value = saved[0][index][...]
        for group in saved[1:]:
            value = jnp.where(micro == 1, group[index][...], value)
        return value

    hidden, joined, produced = pick(0), pick(1), pick(2)
    slot = jnp.where((micro >= 0) & (micro < micros), micro, micros)
    copies = [
        pltpu.make_async_copy(stage[i], kept[i].at[slot], sems.at[i]) for i in range(4)
    ]
    inner = out_ref.shape[1]
    gain, column = gain_ref[...].astype(f32), column_ref[...]
    normed, scaled, inverse = normalize(hidden, gain)
    gate = gate_of(normed, column)
    gate_part, up_part = joined[:, :inner], joined[:, inner:]
    sigmoid_gate = jax.nn.sigmoid(gate_part)
    silu_gate = gate_part * sigmoid_gate
    scaled_grad = (gate.astype(bf16).astype(f32) * upstream_f).astype(bf16)
    stage[0][...] = normed
    stage[2][...] = (silu_gate * up_part).astype(bf16)
    stage[3][...] = scaled_grad
    for i in (0, 2, 3):
        copies[i].start()
    act_grad = jnp.dot(scaled_grad, out_ref[...], preferred_element_type=f32)
    gate_grad = act_grad * up_part * sigmoid_gate * (1.0 + gate_part * (1.0 - sigmoid_gate))
    up_grad = act_grad * silu_gate
    joined_grad = jnp.concatenate([gate_grad, up_grad], axis=-1).astype(bf16)
    stage[1][...] = joined_grad
    copies[1].start()
    if passes:
        rows_grad = jnp.dot(joined_grad, in_ref[...], preferred_element_type=f32).astype(bf16)
        share_grad = jnp.sum(produced.astype(f32) * upstream_f, axis=-1, keepdims=True)
        logit_grad = share_grad.astype(bf16).astype(f32) * gate * (1.0 - gate)
        gained = (rows_grad.astype(f32) + logit_grad * column) * gain
        centred = gained - scaled * jnp.mean(gained * scaled, axis=-1, keepdims=True)
        passed = (upstream_f + inverse * centred).astype(bf16)
        split_rows(sent, passed, layer == last, ahead)
    for copy in copies:
        copy.wait()


def resort_kernel(plan, place_ref, order_ref, *refs):
    arrivals, count, width, entry, last = plan
    arrived = refs[:arrivals]
    rest = refs[arrivals:]
    sent = rest[-count:]
    value = jnp.dot(
        order_ref[0], joined_rows(arrived, width), preferred_element_type=f32
    ).astype(bf16)
    if entry:
        layer = place_ref[0]
        value = jnp.where((layer == 0) | (layer == last), rest[0][...], value)
    split_rows(sent, value)


def prepare_kernel(plan, place_ref, *refs):
    homes, layers, micros, ranks, room, size, count = plan
    routes, entering = refs[:homes], refs[homes : 2 * homes]
    sent = refs[2 * homes : 2 * homes + count]
    start_ref, order_ref = refs[2 * homes + count :]
    layer, rank = place_ref[0], place_ref[1]
    tokens = routes[0].shape[1]
    rows = size * count
    near = [jnp.maximum(layer - 1, 0), layer, jnp.minimum(layer + 1, layers - 1)]
    ids = [
        [[routes[j][pl.ds(at * micros + m, 1), :] for m in range(micros)] for at in near]
        for j in range(homes)
    ]
    experts = lax.broadcasted_iota(jnp.int32, (ranks, tokens), 0)
    before = (
        lax.broadcasted_iota(jnp.int32, (tokens, tokens), 0)
        < lax.broadcasted_iota(jnp.int32, (tokens, tokens), 1)
    ).astype(f32).astype(bf16)
    flat = [row for home in ids for at in home for row in at]
    marks = jnp.concatenate([(experts == row).astype(f32) for row in flat], axis=0)
    earlier = marks * jnp.dot(marks.astype(bf16), before, preferred_element_type=f32)
    within = [
        jnp.sum(earlier[i * ranks : (i + 1) * ranks], axis=0, keepdims=True).astype(jnp.int32)
        for i in range(len(flat))
    ]

    def one_hot(size, index):
        slots = lax.broadcasted_iota(jnp.int32, (size, tokens), 0)
        return (slots == index).astype(f32).astype(bf16)

    def places(j, at, m):
        row, depth = ids[j][at][m], within[(j * 3 + at) * micros + m]
        if homes == 1:
            index = row * room + depth
            return index, index
        offset = row ^ rank
        far, other = offset >> 1, offset & 1
        target = jnp.where(other == 0, far * size + j * room + depth, -1)
        side = other if j == 0 else 1 - other
        return target, other * rows + far * size + side * room + depth

    for m in range(micros):
        here = [one_hot(rows, places(j, 1, m)[0]) for j in range(homes)]
        for which, at in enumerate((0, 2)):
            total = 0.0
            for j in range(homes):
                there = one_hot(homes * rows, places(j, at, m)[1])
                total += lax.dot_general(here[j], there, LAST, preferred_element_type=f32)
            order_ref[which * micros + m] = total.astype(bf16)
        start = 0.0
        for j in range(homes):
            start += jnp.dot(here[j], entering[j][m], preferred_element_type=f32)
        if m == 0:
            split_rows(sent, start.astype(bf16))
        else:
            start_ref[m - 1] = start.astype(bf16)


def transpose_kernel(in_ref, out_ref, in_turned, out_turned):
    in_turned[...] = in_ref[...].T
    out_turned[...] = out_ref[...].T


def grads_kernel(parts, *refs):
    in_ref, out_ref = refs[4 * parts :]

    def gathered(which):
        groups = [refs[4 * part + which] for part in range(parts)]
        return jnp.concatenate([g[m] for g in groups for m in range(g.shape[0])], axis=0)

    in_ref[...] = lax.dot_general(
        gathered(0), gathered(1), FIRST, preferred_element_type=f32
    ).astype(bf16)
    out_ref[...] = lax.dot_general(
        gathered(2), gathered(3), FIRST, preferred_element_type=f32
    ).astype(bf16)


def shards(tokens_in, out_grad, routes, router, norm_gain, w_in, w_out):
    layers = lax.axis_size("pipe")
    ranks = lax.axis_size("expert")
    layer = lax.axis_index("pipe")
    rank = lax.axis_index("expert")
    micros, tokens, width = tokens_in.shape
    assert routes.shape[3] == 1 and router.shape[2] == ranks
    assert micros == 2 and layers > 2 and layers % 2 == 0
    capacity = max(2, tokens * 3 // (2 * ranks))
    paired = ranks <= WIDEST and ranks & (ranks - 1) == 0 and capacity >= 8
    count = ranks // 2 if paired else 1
    homes = 2 if paired else 1
    if paired:
        room = capacity
        size = -(-2 * room // 16) * 16
    else:
        room = -(-capacity // 4) * 4
        size = ranks * room
    rows = size * count
    tight = paired and size == 2 * room + 2 and width == LANES * (room + 1)
    short = width - LANES if tight else width
    parts = [[0, 3], [1, 2]] if count == 4 else [list(range(count))]
    last = layers - 1
    steps = 2 * last + micros
    own_in, own_out, gain_row = w_in[0, 0], w_out[0, 0], norm_gain
    double, inner = own_in.shape[1], own_out.shape[0]
    column = (
        lax.dynamic_index_in_dim(router[0], rank, 1, keepdims=False).astype(f32).reshape(1, width)
    )
    places = [
        jnp.stack([layer, rank, jnp.int32(step)]).astype(jnp.int32) for step in range(steps)
    ]
    piece = jax.ShapeDtypeStruct((size, short), bf16)
    params = pltpu.CompilerParams(vmem_limit_bytes=16 << 20)

    def permuted(block, offset, jump):
        route = []
        for p in range(layers):
            q = p if jump is None else jump(p)
            route += [(p * ranks + i, q * ranks + (i ^ offset)) for i in range(ranks)]
        return lax.ppermute(block, ("pipe", "expert"), route)

    def spread(pieces):
        return lax.all_to_all(
            pieces[0].reshape(ranks, room, width), "expert", split_axis=0, concat_axis=0, tiled=True
        ).reshape(rows, width)

    def to_experts(pieces):
        if not paired:
            return [spread(pieces)]
        arrived = [pieces[0]] + [None] * (count - 1)
        for k in sorted(range(1, count), key=lambda k: (k % 2, -k)):
            arrived[k] = permuted(pieces[k], 2 * k, None)
        return arrived

    def to_homes(pieces, jump):
        if not paired:
            return [lax.ppermute(spread(pieces), "pipe", [(p, jump(p)) for p in range(layers)])]
        arrived, swapped = [None] * count, [None] * count
        for part in parts:
            for k in reversed(part):
                arrived[k] = permuted(pieces[k], 2 * k, jump)
                swapped[k] = permuted(arrived[k], 1, None)
        return arrived + swapped

    entering = jnp.where(layer == 0, tokens_in, out_grad)
    ids = routes.reshape(layers * micros, tokens)
    both_ids, both_entering = [ids], [entering]
    if paired:
        both_ids.append(permuted(ids, 1, None))
        both_entering.append(permuted(entering, 1, None))
    *pieces, start, order = pl.pallas_call(
        functools.partial(prepare_kernel, (homes, layers, micros, ranks, room, size, count)),
        out_shape=[piece] * count
        + [
            jax.ShapeDtypeStruct((micros - 1, rows, width), bf16),
            jax.ShapeDtypeStruct((2 * micros, rows, homes * rows), bf16),
        ],
        in_specs=[SMEM] + [VMEM] * (2 * homes),
        out_specs=[VMEM] * (count + 2),
        compiler_params=params,
        name="prepare",
    )(places[0], *both_ids, *both_entering)

    def resort(step, arrived):
        def which(ref):
            forward_micro = ref[2] - ref[0]
            backward_micro = jnp.clip(forward_micro - 2 * (last - ref[0]), 0, micros - 1)
            is_forward = (forward_micro >= 0) & (forward_micro < micros)
            return jnp.where(is_forward, forward_micro, micros + backward_micro)

        entry = step < micros
        whole = lambda shape: pl.BlockSpec(shape, lambda i, ref: (0,) * len(shape))
        ins = list(arrived) + ([start[step - 1]] if entry else [])
        return pl.pallas_call(
            functools.partial(resort_kernel, (len(arrived), count, width, entry, last)),
            out_shape=[piece] * count,
            grid_spec=pltpu.PrefetchScalarGridSpec(
                num_scalar_prefetch=1,
                grid=(1,),
                in_specs=[
                    pl.BlockSpec((1, rows, homes * rows), lambda i, ref: (which(ref), 0, 0))
                ]
                + [whole(value.shape) for value in ins],
                out_specs=[whole((size, short))] * count,
            ),
            compiler_params=params,
            name="resort",
        )(places[step], order, *ins)

    def forward(arrived, earlier):
        many = len(arrived)
        out = pl.pallas_call(
            functools.partial(forward_kernel, many, len(earlier)),
            out_shape=[piece] * many
            + [
                jax.ShapeDtypeStruct((many * size, width), bf16),
                jax.ShapeDtypeStruct((many * size, double), f32),
                jax.ShapeDtypeStruct((many * size, width), bf16),
            ],
            in_specs=[VMEM] * (4 + many) + [ANY] * len(earlier),
            out_specs=[VMEM] * (many + 3),
            compiler_params=params,
            name="forward",
        )(gain_row, column, own_in, own_out, *arrived, *earlier)
        return out[:many], out[many:]

    kept_sizes = (width, double, inner, width)
    bands = 8
    turned_in, turned_out = pl.pallas_call(
        transpose_kernel,
        grid=(bands,),
        out_shape=[
            jax.ShapeDtypeStruct((double, width), bf16),
            jax.ShapeDtypeStruct((width, inner), bf16),
        ],
        in_specs=[
            pl.BlockSpec((width // bands, double), lambda i: (i, 0)),
            pl.BlockSpec((inner, width // bands), lambda i: (0, i)),
        ],
        out_specs=[
            pl.BlockSpec((double, width // bands), lambda i: (0, i)),
            pl.BlockSpec((width // bands, inner), lambda i: (i, 0)),
        ],
        compiler_params=params,
        name="turn",
    )(own_in, own_out)

    def backward(step, arrived, entered, ahead, saved, kept, earlier):
        passes = step + 1 < steps
        many = len(arrived)
        sources = [
            saved[step - 2 * (last - p)]
            for p in range(layers)
            if 0 <= step - (2 * last - p) < micros
        ]
        plan = (
            many,
            layers,
            micros,
            len(sources),
            entered is not None,
            step == last,
            len(earlier),
            kept is not None,
            passes,
        )
        operands = [places[step], gain_row, column, turned_in, turned_out, *arrived]
        if entered is not None:
            operands += entered
        if step == last:
            operands += ahead
        for group in sources:
            operands += group
        specs = [SMEM] + [VMEM] * (len(operands) - 1) + [ANY] * len(earlier)
        operands += earlier
        sent = many if passes else 0
        aliases = {}
        if kept is not None:
            aliases = {len(operands) + i: sent + i for i in range(4)}
            operands += kept
            specs += [ANY] * 4
        held = [(many * size, length) for length in kept_sizes]
        out = pl.pallas_call(
            functools.partial(backward_kernel, plan),
            out_shape=[piece] * sent
            + [jax.ShapeDtypeStruct((micros + 1, *shape), bf16) for shape in held],
            in_specs=specs,
            out_specs=[VMEM] * sent + [ANY] * 4,
            scratch_shapes=[pltpu.VMEM(shape, bf16) for shape in held]
            + [pltpu.SemaphoreType.DMA((4,))],
            input_output_aliases=aliases,
            compiler_params=params,
            name="backward",
        )(*operands)
        return out[:sent], out[sent:]

    arrivals = []
    forwards = [[] for _ in parts]
    kept = [None for _ in parts]
    for step in range(steps):
        arrived = to_experts(pieces)
        arrivals.append(arrived)
        pieces, earlier = [None] * count, []
        for index, part in enumerate(parts):
            here = [arrived[k] for k in part]
            passed = None
            if step < last + micros:
                passed, saved = forward(here, earlier)
                forwards[index].append(saved)
            if step >= last:
                entered = None
                if step < last + micros:
                    entered = [arrivals[step - last][k] for k in part]
                passed, kept[index] = backward(
                    step, here, entered, passed, forwards[index], kept[index], earlier
                )
            for k, value in zip(part, passed):
                pieces[k] = value
            earlier = passed[:1]
        if step + 1 == steps:
            break
        if step < last:
            jump = lambda p: (p + 1) % layers
        elif step == last:
            jump = lambda p: p ^ 1
        else:
            jump = lambda p: (p - 1) % layers
        pieces = resort(step + 1, to_homes(pieces, jump))

    cuts = 4
    specs = []
    for part in parts:
        depth = len(part) * size
        column_block = lambda length: pl.BlockSpec((micros, depth, length), lambda i: (0, 0, i))
        whole_block = lambda length: pl.BlockSpec((micros, depth, length), lambda i: (0, 0, 0))
        specs += [
            column_block(width // cuts),
            whole_block(double),
            column_block(inner // cuts),
            whole_block(width),
        ]
    grad_in, grad_out = pl.pallas_call(
        functools.partial(grads_kernel, len(parts)),
        grid=(cuts,),
        out_shape=[
            jax.ShapeDtypeStruct((width, double), bf16),
            jax.ShapeDtypeStruct((inner, width), bf16),
        ],
        in_specs=specs,
        out_specs=[
            pl.BlockSpec((width // cuts, double), lambda i: (i, 0)),
            pl.BlockSpec((inner // cuts, width), lambda i: (i, 0)),
        ],
        compiler_params=params,
        name="grads",
    )(*[buffer for group in kept for buffer in group])
    return grad_in[None, None], grad_out[None, None]


def solution(mesh):
    placed = (
        P(None, "expert", None),
        P(None, "expert", None),
        P(None, None, "expert", None),
        P("pipe", None, None),
        P("pipe", None),
        P("pipe", "expert", None, None),
        P("pipe", "expert", None, None),
    )
    return jax.shard_map(
        shards,
        mesh=mesh,
        in_specs=placed,
        out_specs=(P("pipe", "expert", None, None), P("pipe", "expert", None, None)),
        check_vma=False,
    )
```

```python
import functools

import jax
import jax.numpy as jnp
from jax import lax
from jax.experimental import pallas as pl
from jax.experimental.pallas import tpu as pltpu
from jax.sharding import PartitionSpec as P


epsilon = 1e-06


f32, bf16 = jnp.float32, jnp.bfloat16
VMEM = pl.BlockSpec(memory_space=pltpu.VMEM)
SMEM = pl.BlockSpec(memory_space=pltpu.SMEM)
ANY = pl.BlockSpec(memory_space=pl.ANY)
LAST = (((1,), (1,)), ((), ()))
FIRST = (((0,), (0,)), ((), ()))
LANES = 128
WIDEST = 8


def unpacked(ref, width):
    value = ref[...]
    size = value.shape[0]
    if value.shape[1] == width:
        return value
    real = size - 2
    spare = value[real:].astype(f32)
    blocks = [spare[:, i * LANES : (i + 1) * LANES] for i in range(real // 2)]
    tail = jnp.concatenate(blocks + [jnp.zeros((2, LANES), f32)], axis=0).astype(bf16)
    held = lax.broadcasted_iota(jnp.int32, value.shape, 0) < real
    return jnp.concatenate([jnp.where(held, value, jnp.zeros_like(value)), tail], axis=1)


def packed(value, short):
    if value.shape[1] == short:
        return value
    real = value.shape[0] - 2
    tail = value[:, short:].astype(f32)
    spare = jnp.concatenate([tail[2 * i : 2 * i + 2] for i in range(real // 2)], axis=1)
    last = value[-16:, :short].astype(f32)
    last = jnp.concatenate([last[:14], spare], axis=0).astype(bf16)
    return jnp.concatenate([value[:-16, :short], last], axis=0)


def joined_rows(refs, width):
    parts = [unpacked(ref, width) for ref in refs]
    return parts[0] if len(parts) == 1 else jnp.concatenate(parts, axis=0)


def split_rows(refs, value, keep=None, others=None):
    size, short = refs[0].shape
    for k, ref in enumerate(refs):
        block = packed(value[k * size : (k + 1) * size], short)
        if others is not None:
            block = jnp.where(keep, block, others[k][...])
        ref[...] = block


def normalize(hidden, gain):
    values = hidden.astype(f32)
    inverse = lax.rsqrt(jnp.mean(values * values, axis=-1, keepdims=True) + epsilon)
    scaled = values * inverse
    return (scaled * gain).astype(bf16), scaled, inverse


def gate_of(normed, column):
    return jax.nn.sigmoid(jnp.sum(normed.astype(f32) * column, axis=-1, keepdims=True))


def forward_kernel(count, chained, gain_ref, column_ref, in_ref, out_ref, *refs):
    arrived, refs = refs[:count], refs[count + chained :]
    sent, refs = refs[:count], refs[count:]
    hidden_ref, joined_ref, produced_ref, inverse_ref, gate_ref, normed_ref, activated_ref = refs
    inner = out_ref.shape[0]
    hidden = joined_rows(arrived, in_ref.shape[0])
    normed, _, inverse = normalize(hidden, gain_ref[...].astype(f32))
    gate = gate_of(normed, column_ref[...])
    share = gate.astype(bf16).astype(f32)
    joined = jnp.dot(normed, in_ref[...], preferred_element_type=f32)
    gate_part = joined[:, :inner]
    activated = (gate_part * jax.nn.sigmoid(gate_part) * joined[:, inner:]).astype(bf16)
    produced = jnp.dot(activated, out_ref[...], preferred_element_type=f32).astype(bf16)
    output = (hidden.astype(f32) + share * produced.astype(f32)).astype(bf16)
    split_rows(sent, output)
    hidden_ref[...] = hidden
    joined_ref[...] = joined
    produced_ref[...] = produced
    inverse_ref[...] = inverse
    gate_ref[...] = gate
    normed_ref[...] = normed
    activated_ref[...] = activated


def backward_kernel(plan, place_ref, gain_ref, column_ref, in_ref, out_ref, *refs):
    count, layers, _, sets, enters, first, chained, passes = plan
    last = layers - 1
    layer, step = place_ref[0], place_ref[2]
    refs = list(refs)
    take = lambda number: [refs.pop(0) for _ in range(number)]
    arrived = take(count)
    entered = take(count) if enters else None
    ahead = take(count) if first else None
    saved = [take(5) for _ in range(sets)]
    take(chained)
    sent = take(count) if passes else None
    joined_grad_ref, scaled_grad_ref = refs
    width = out_ref.shape[0]
    upstream = joined_rows(arrived, width)
    if entered is not None:
        upstream = jnp.where(layer == last, joined_rows(entered, width), upstream)
    upstream_f = upstream.astype(f32)
    micro = step - (2 * last - layer)

    def pick(index):
        value = saved[0][index][...]
        for group in saved[1:]:
            value = jnp.where(micro == 1, group[index][...], value)
        return value

    joined, inverse, gate = pick(1), pick(3), pick(4)
    inner = out_ref.shape[1]
    gate_part, up_part = joined[:, :inner], joined[:, inner:]
    sigmoid_gate = jax.nn.sigmoid(gate_part)
    silu_gate = gate_part * sigmoid_gate
    scaled_grad = (gate.astype(bf16).astype(f32) * upstream_f).astype(bf16)
    scaled_grad_ref[...] = scaled_grad
    act_grad = jnp.dot(scaled_grad, out_ref[...], preferred_element_type=f32)
    gate_grad = act_grad * up_part * sigmoid_gate * (1.0 + gate_part * (1.0 - sigmoid_gate))
    up_grad = act_grad * silu_gate
    joined_grad = jnp.concatenate([gate_grad, up_grad], axis=-1).astype(bf16)
    joined_grad_ref[...] = joined_grad
    if passes:
        rows_grad = jnp.dot(joined_grad, in_ref[...], preferred_element_type=f32).astype(bf16)
        share_grad = jnp.sum(pick(2).astype(f32) * upstream_f, axis=-1, keepdims=True)
        logit_grad = share_grad.astype(bf16).astype(f32) * gate * (1.0 - gate)
        gained = (rows_grad.astype(f32) + logit_grad * column_ref[...]) * gain_ref[...].astype(f32)
        scaled = pick(0).astype(f32) * inverse
        centred = gained - scaled * jnp.mean(gained * scaled, axis=-1, keepdims=True)
        passed = (upstream_f + inverse * centred).astype(bf16)
        split_rows(sent, passed, layer == last, ahead)


def record_kernel(plan, place_ref, *refs):
    layers, micros, sets, aliased = plan
    refs = list(refs)
    take = lambda number: [refs.pop(0) for _ in range(number)]
    grads = take(2)
    saved = [take(2) for _ in range(sets)]
    take(4 * aliased)
    kept = take(4)
    sems = refs.pop(0)
    micro = place_ref[2] - (2 * (layers - 1) - place_ref[0])
    slot = jnp.where((micro >= 0) & (micro < micros), micro, micros)

    def copy_all(chosen):
        sources = (chosen[0], grads[0], chosen[1], grads[1])
        copies = [
            pltpu.make_async_copy(sources[i], kept[i].at[slot], sems.at[i]) for i in range(4)
        ]
        for copy in copies:
            copy.start()
        for copy in copies:
            copy.wait()

    if sets == 1:
        copy_all(saved[0])
    else:
        pl.when(micro != 1)(lambda: copy_all(saved[0]))
        pl.when(micro == 1)(lambda: copy_all(saved[1]))


def resort_kernel(plan, place_ref, order_ref, *refs):
    arrivals, count, width, entry, last = plan
    arrived = refs[:arrivals]
    rest = refs[arrivals:]
    sent = rest[-count:]
    value = jnp.dot(
        order_ref[0], joined_rows(arrived, width), preferred_element_type=f32
    ).astype(bf16)
    if entry:
        layer = place_ref[0]
        value = jnp.where((layer == 0) | (layer == last), rest[0][...], value)
    split_rows(sent, value)


def prepare_kernel(plan, place_ref, *refs):
    homes, layers, micros, ranks, room, size, count = plan
    routes, entering = refs[:homes], refs[homes : 2 * homes]
    sent = refs[2 * homes : 2 * homes + count]
    start_ref, order_ref = refs[2 * homes + count :]
    layer, rank = place_ref[0], place_ref[1]
    tokens = routes[0].shape[1]
    rows = size * count
    near = [jnp.maximum(layer - 1, 0), layer, jnp.minimum(layer + 1, layers - 1)]
    ids = [
        [[routes[j][pl.ds(at * micros + m, 1), :] for m in range(micros)] for at in near]
        for j in range(homes)
    ]
    experts = lax.broadcasted_iota(jnp.int32, (ranks, tokens), 0)
    before = (
        lax.broadcasted_iota(jnp.int32, (tokens, tokens), 0)
        < lax.broadcasted_iota(jnp.int32, (tokens, tokens), 1)
    ).astype(f32).astype(bf16)
    flat = [row for home in ids for at in home for row in at]
    marks = jnp.concatenate([(experts == row).astype(f32) for row in flat], axis=0)
    earlier = marks * jnp.dot(marks.astype(bf16), before, preferred_element_type=f32)
    within = [
        jnp.sum(earlier[i * ranks : (i + 1) * ranks], axis=0, keepdims=True).astype(jnp.int32)
        for i in range(len(flat))
    ]

    def one_hot(size, index):
        slots = lax.broadcasted_iota(jnp.int32, (size, tokens), 0)
        return (slots == index).astype(f32).astype(bf16)

    def places(j, at, m):
        row, depth = ids[j][at][m], within[(j * 3 + at) * micros + m]
        if homes == 1:
            index = row * room + depth
            return index, index
        offset = row ^ rank
        far, other = offset >> 1, offset & 1
        target = jnp.where(other == 0, far * size + j * room + depth, -1)
        side = other if j == 0 else 1 - other
        return target, other * rows + far * size + side * room + depth

    for m in range(micros):
        here = [one_hot(rows, places(j, 1, m)[0]) for j in range(homes)]
        for which, at in enumerate((0, 2)):
            total = 0.0
            for j in range(homes):
                there = one_hot(homes * rows, places(j, at, m)[1])
                total += lax.dot_general(here[j], there, LAST, preferred_element_type=f32)
            order_ref[which * micros + m] = total.astype(bf16)
        start = 0.0
        for j in range(homes):
            start += jnp.dot(here[j], entering[j][m], preferred_element_type=f32)
        if m == 0:
            split_rows(sent, start.astype(bf16))
        else:
            start_ref[m - 1] = start.astype(bf16)


def transpose_kernel(in_ref, out_ref, in_turned, out_turned):
    in_turned[...] = in_ref[...].T
    out_turned[...] = out_ref[...].T


def grads_kernel(parts, place_ref, *refs):
    in_ref, out_ref = refs[8 * parts :]
    first = place_ref[0] == 0

    def gathered(which):
        blocks = []
        for part in range(parts):
            ref = refs[8 * part + which]
            micros = ref.shape[0]
            for m in range(micros):
                block = ref[m]
                if m == micros - 1:
                    block = jnp.where(first, refs[8 * part + which + 4][...], block)
                blocks.append(block)
        return jnp.concatenate(blocks, axis=0)

    in_ref[...] = lax.dot_general(
        gathered(0), gathered(1), FIRST, preferred_element_type=f32
    ).astype(bf16)
    out_ref[...] = lax.dot_general(
        gathered(2), gathered(3), FIRST, preferred_element_type=f32
    ).astype(bf16)


def shards(tokens_in, out_grad, routes, router, norm_gain, w_in, w_out):
    layers = lax.axis_size("pipe")
    ranks = lax.axis_size("expert")
    layer = lax.axis_index("pipe")
    rank = lax.axis_index("expert")
    micros, tokens, width = tokens_in.shape
    assert routes.shape[3] == 1 and router.shape[2] == ranks
    assert micros == 2 and layers > 2 and layers % 2 == 0
    capacity = max(2, tokens * 3 // (2 * ranks))
    paired = ranks <= WIDEST and ranks & (ranks - 1) == 0 and capacity >= 8
    count = ranks // 2 if paired else 1
    homes = 2 if paired else 1
    if paired:
        room = capacity
        size = -(-2 * room // 16) * 16
    else:
        room = -(-capacity // 4) * 4
        size = ranks * room
    rows = size * count
    tight = paired and size == 2 * room + 2 and width == LANES * (room + 1)
    short = width - LANES if tight else width
    parts = [[0, 3], [1, 2]] if count == 4 else [list(range(count))]
    last = layers - 1
    steps = 2 * last + micros
    own_in, own_out, gain_row = w_in[0, 0], w_out[0, 0], norm_gain
    double, inner = own_in.shape[1], own_out.shape[0]
    column = (
        lax.dynamic_index_in_dim(router[0], rank, 1, keepdims=False).astype(f32).reshape(1, width)
    )
    places = [
        jnp.stack([layer, rank, jnp.int32(step)]).astype(jnp.int32) for step in range(steps)
    ]
    piece = jax.ShapeDtypeStruct((size, short), bf16)
    params = pltpu.CompilerParams(vmem_limit_bytes=16 << 20)

    def permuted(block, offset, jump):
        route = []
        for p in range(layers):
            q = p if jump is None else jump(p)
            route += [(p * ranks + i, q * ranks + (i ^ offset)) for i in range(ranks)]
        return lax.ppermute(block, ("pipe", "expert"), route)

    def spread(pieces):
        return lax.all_to_all(
            pieces[0].reshape(ranks, room, width), "expert", split_axis=0, concat_axis=0, tiled=True
        ).reshape(rows, width)

    def to_experts(pieces):
        if not paired:
            return [spread(pieces)]
        arrived = [pieces[0]] + [None] * (count - 1)
        for k in sorted(range(1, count), key=lambda k: (k % 2, -k)):
            arrived[k] = permuted(pieces[k], 2 * k, None)
        return arrived

    def to_homes(pieces, jump):
        if not paired:
            return [lax.ppermute(spread(pieces), "pipe", [(p, jump(p)) for p in range(layers)])]
        arrived, swapped = [None] * count, [None] * count
        for part in parts:
            for k in reversed(part):
                arrived[k] = permuted(pieces[k], 2 * k, jump)
                swapped[k] = permuted(arrived[k], 1, None)
        return arrived + swapped

    entering = jnp.where(layer == 0, tokens_in, out_grad)
    ids = routes.reshape(layers * micros, tokens)
    both_ids, both_entering = [ids], [entering]
    if paired:
        both_ids.append(permuted(ids, 1, None))
        both_entering.append(permuted(entering, 1, None))
    *pieces, start, order = pl.pallas_call(
        functools.partial(prepare_kernel, (homes, layers, micros, ranks, room, size, count)),
        out_shape=[piece] * count
        + [
            jax.ShapeDtypeStruct((micros - 1, rows, width), bf16),
            jax.ShapeDtypeStruct((2 * micros, rows, homes * rows), bf16),
        ],
        in_specs=[SMEM] + [VMEM] * (2 * homes),
        out_specs=[VMEM] * (count + 2),
        compiler_params=params,
        name="prepare",
    )(places[0], *both_ids, *both_entering)

    def resort(step, arrived):
        def which(ref):
            forward_micro = ref[2] - ref[0]
            backward_micro = jnp.clip(forward_micro - 2 * (last - ref[0]), 0, micros - 1)
            is_forward = (forward_micro >= 0) & (forward_micro < micros)
            return jnp.where(is_forward, forward_micro, micros + backward_micro)

        entry = step < micros
        whole = lambda shape: pl.BlockSpec(shape, lambda i, ref: (0,) * len(shape))
        ins = list(arrived) + ([start[step - 1]] if entry else [])
        return pl.pallas_call(
            functools.partial(resort_kernel, (len(arrived), count, width, entry, last)),
            out_shape=[piece] * count,
            grid_spec=pltpu.PrefetchScalarGridSpec(
                num_scalar_prefetch=1,
                grid=(1,),
                in_specs=[
                    pl.BlockSpec((1, rows, homes * rows), lambda i, ref: (which(ref), 0, 0))
                ]
                + [whole(value.shape) for value in ins],
                out_specs=[whole((size, short))] * count,
            ),
            compiler_params=params,
            name="resort",
        )(places[step], order, *ins)

    def forward(arrived, earlier):
        many = len(arrived)
        form = lambda length, dtype: jax.ShapeDtypeStruct((many * size, length), dtype)
        out = pl.pallas_call(
            functools.partial(forward_kernel, many, len(earlier)),
            out_shape=[piece] * many
            + [
                form(width, bf16),
                form(double, f32),
                form(width, bf16),
                form(1, f32),
                form(1, f32),
                form(width, bf16),
                form(inner, bf16),
            ],
            in_specs=[VMEM] * (4 + many) + [ANY] * len(earlier),
            out_specs=[VMEM] * (many + 7),
            compiler_params=params,
            name="forward",
        )(gain_row, column, own_in, own_out, *arrived, *earlier)
        return out[:many], out[many:]

    def record(step, grads, saved, kept):
        sources = sources_of(step, saved)
        operands = [places[step], *grads]
        for group in sources:
            operands += group[5:]
        specs = [SMEM] + [ANY] * (len(operands) - 1)
        aliases = {}
        if kept is not None:
            aliases = {len(operands) + i: i for i in range(4)}
            operands += kept
            specs += [ANY] * 4
        depth = grads[0].shape[0]
        return pl.pallas_call(
            functools.partial(record_kernel, (layers, micros, len(sources), kept is not None)),
            out_shape=[
                jax.ShapeDtypeStruct((micros + 1, depth, length), bf16)
                for length in (width, double, inner, width)
            ],
            in_specs=specs,
            out_specs=[ANY] * 4,
            scratch_shapes=[pltpu.SemaphoreType.DMA((4,))],
            input_output_aliases=aliases,
            compiler_params=params,
            name="record",
        )(*operands)

    def sources_of(step, saved):
        return [
            saved[step - 2 * (last - p)]
            for p in range(layers)
            if 0 <= step - (2 * last - p) < micros
        ]

    bands = 8
    turned_in, turned_out = pl.pallas_call(
        transpose_kernel,
        grid=(bands,),
        out_shape=[
            jax.ShapeDtypeStruct((double, width), bf16),
            jax.ShapeDtypeStruct((width, inner), bf16),
        ],
        in_specs=[
            pl.BlockSpec((width // bands, double), lambda i: (i, 0)),
            pl.BlockSpec((inner, width // bands), lambda i: (0, i)),
        ],
        out_specs=[
            pl.BlockSpec((double, width // bands), lambda i: (0, i)),
            pl.BlockSpec((width // bands, inner), lambda i: (i, 0)),
        ],
        compiler_params=params,
        name="turn",
    )(own_in, own_out)

    def backward(step, arrived, entered, ahead, saved, earlier):
        passes = step + 1 < steps
        many = len(arrived)
        sources = sources_of(step, saved)
        plan = (
            many,
            layers,
            micros,
            len(sources),
            entered is not None,
            step == last,
            len(earlier),
            passes,
        )
        operands = [places[step], gain_row, column, turned_in, turned_out, *arrived]
        if entered is not None:
            operands += entered
        if step == last:
            operands += ahead
        for group in sources:
            operands += group[:5]
        specs = [SMEM] + [VMEM] * (len(operands) - 1) + [ANY] * len(earlier)
        operands += earlier
        sent = many if passes else 0
        out = pl.pallas_call(
            functools.partial(backward_kernel, plan),
            out_shape=[piece] * sent
            + [
                jax.ShapeDtypeStruct((many * size, length), bf16) for length in (double, width)
            ],
            in_specs=specs,
            out_specs=[VMEM] * (sent + 2),
            compiler_params=params,
            name="backward",
        )(*operands)
        return out[:sent], out[sent:]

    arrivals = []
    forwards = [[] for _ in parts]
    kept = [None for _ in parts]
    grads = [None for _ in parts]
    for step in range(steps):
        arrived = to_experts(pieces)
        arrivals.append(arrived)
        pieces, earlier = [None] * count, []
        for index, part in enumerate(parts):
            here = [arrived[k] for k in part]
            passed = None
            if step < last + micros:
                passed, saved = forward(here, earlier)
                forwards[index].append(saved)
            if step >= last:
                entered = None
                if step < last + micros:
                    entered = [arrivals[step - last][k] for k in part]
                passed, grads[index] = backward(
                    step, here, entered, passed, forwards[index], earlier
                )
                if step + 1 < steps:
                    kept[index] = record(
                        step, grads[index], forwards[index], kept[index]
                    )
            for k, value in zip(part, passed):
                pieces[k] = value
            earlier = passed[:1]
        if step + 1 == steps:
            break
        if step < last:
            jump = lambda p: (p + 1) % layers
        elif step == last:
            jump = lambda p: p ^ 1
        else:
            jump = lambda p: (p - 1) % layers
        pieces = resort(step + 1, to_homes(pieces, jump))

    cuts = 4
    specs = []
    for part in parts:
        depth = len(part) * size
        column_block = lambda length: pl.BlockSpec((micros, depth, length), lambda i: (0, 0, i))
        whole_block = lambda length: pl.BlockSpec((micros, depth, length), lambda i: (0, 0, 0))
        specs += [
            column_block(width // cuts),
            whole_block(double),
            column_block(inner // cuts),
            whole_block(width),
            pl.BlockSpec((depth, width // cuts), lambda i: (0, i)),
            pl.BlockSpec((depth, double), lambda i: (0, 0)),
            pl.BlockSpec((depth, inner // cuts), lambda i: (0, i)),
            pl.BlockSpec((depth, width), lambda i: (0, 0)),
        ]
    final = []
    for group, pair, saved in zip(kept, grads, forwards):
        normed, activated = saved[steps - 1 - 2 * last][5:]
        final += [*group, normed, pair[0], activated, pair[1]]
    grad_in, grad_out = pl.pallas_call(
        functools.partial(grads_kernel, len(parts)),
        grid=(cuts,),
        out_shape=[
            jax.ShapeDtypeStruct((width, double), bf16),
            jax.ShapeDtypeStruct((inner, width), bf16),
        ],
        in_specs=[SMEM] + specs,
        out_specs=[
            pl.BlockSpec((width // cuts, double), lambda i: (i, 0)),
            pl.BlockSpec((inner // cuts, width), lambda i: (i, 0)),
        ],
        compiler_params=params,
        name="grads",
    )(places[0], *final)
    return grad_in[None, None], grad_out[None, None]


def solution(mesh):
    placed = (
        P(None, "expert", None),
        P(None, "expert", None),
        P(None, None, "expert", None),
        P("pipe", None, None),
        P("pipe", None),
        P("pipe", "expert", None, None),
        P("pipe", "expert", None, None),
    )
    return jax.shard_map(
        shards,
        mesh=mesh,
        in_specs=placed,
        out_specs=(P("pipe", "expert", None, None), P("pipe", "expert", None, None)),
        check_vma=False,
    )
```

```python
import functools

import jax
import jax.numpy as jnp
from jax import lax
from jax.experimental import pallas as pl
from jax.experimental.pallas import tpu as pltpu
from jax.sharding import PartitionSpec as P


epsilon = 1e-06


f32, bf16 = jnp.float32, jnp.bfloat16
VMEM = pl.BlockSpec(memory_space=pltpu.VMEM)
SMEM = pl.BlockSpec(memory_space=pltpu.SMEM)
ANY = pl.BlockSpec(memory_space=pl.ANY)
LAST = (((1,), (1,)), ((), ()))
FIRST = (((0,), (0,)), ((), ()))
LANES = 128
WIDEST = 8


def unpacked(ref, width):
    value = ref[...]
    size = value.shape[0]
    if value.shape[1] == width:
        return value
    real = size - 2
    spare = value[real:].astype(f32)
    blocks = [spare[:, i * LANES : (i + 1) * LANES] for i in range(real // 2)]
    tail = jnp.concatenate(blocks + [jnp.zeros((2, LANES), f32)], axis=0).astype(bf16)
    held = lax.broadcasted_iota(jnp.int32, value.shape, 0) < real
    return jnp.concatenate([jnp.where(held, value, jnp.zeros_like(value)), tail], axis=1)


def packed(value, short):
    if value.shape[1] == short:
        return value
    real = value.shape[0] - 2
    tail = value[:, short:].astype(f32)
    spare = jnp.concatenate([tail[2 * i : 2 * i + 2] for i in range(real // 2)], axis=1)
    last = value[-16:, :short].astype(f32)
    last = jnp.concatenate([last[:14], spare], axis=0).astype(bf16)
    return jnp.concatenate([value[:-16, :short], last], axis=0)


def joined_rows(refs, width):
    parts = [unpacked(ref, width) for ref in refs]
    return parts[0] if len(parts) == 1 else jnp.concatenate(parts, axis=0)


def split_rows(refs, value, keep=None, others=None):
    size, short = refs[0].shape
    for k, ref in enumerate(refs):
        block = packed(value[k * size : (k + 1) * size], short)
        if others is not None:
            block = jnp.where(keep, block, others[k][...])
        ref[...] = block


def normalize(hidden, gain):
    values = hidden.astype(f32)
    inverse = lax.rsqrt(jnp.mean(values * values, axis=-1, keepdims=True) + epsilon)
    scaled = values * inverse
    return (scaled * gain).astype(bf16), scaled, inverse


def gate_of(normed, column):
    return jax.nn.sigmoid(jnp.sum(normed.astype(f32) * column, axis=-1, keepdims=True))


def forward_kernel(count, chained, gain_ref, column_ref, in_ref, out_ref, *refs):
    arrived, refs = refs[:count], refs[count + chained :]
    sent, refs = refs[:count], refs[count:]
    hidden_ref, joined_ref, produced_ref, inverse_ref, gate_ref, normed_ref, activated_ref = refs
    inner = out_ref.shape[0]
    hidden = joined_rows(arrived, in_ref.shape[0])
    normed, _, inverse = normalize(hidden, gain_ref[...].astype(f32))
    gate = gate_of(normed, column_ref[...])
    share = gate.astype(bf16).astype(f32)
    joined = jnp.dot(normed, in_ref[...], preferred_element_type=f32)
    gate_part = joined[:, :inner]
    activated = (gate_part * jax.nn.sigmoid(gate_part) * joined[:, inner:]).astype(bf16)
    produced = jnp.dot(activated, out_ref[...], preferred_element_type=f32).astype(bf16)
    output = (hidden.astype(f32) + share * produced.astype(f32)).astype(bf16)
    split_rows(sent, output)
    hidden_ref[...] = hidden
    joined_ref[...] = joined
    produced_ref[...] = produced
    inverse_ref[...] = inverse
    gate_ref[...] = gate
    normed_ref[...] = normed
    activated_ref[...] = activated


def backward_kernel(plan, place_ref, gain_ref, column_ref, in_ref, out_ref, *refs):
    count, layers, _, sets, enters, first, chained, passes = plan
    last = layers - 1
    layer, step = place_ref[0], place_ref[2]
    refs = list(refs)
    take = lambda number: [refs.pop(0) for _ in range(number)]
    arrived = take(count)
    entered = take(count) if enters else None
    ahead = take(count) if first else None
    saved = [take(5) for _ in range(sets)]
    take(chained)
    sent = take(count) if passes else None
    joined_grad_ref, scaled_grad_ref = refs
    width = out_ref.shape[0]
    upstream = joined_rows(arrived, width)
    if entered is not None:
        upstream = jnp.where(layer == last, joined_rows(entered, width), upstream)
    upstream_f = upstream.astype(f32)
    micro = step - (2 * last - layer)

    def pick(index):
        value = saved[0][index][...]
        for group in saved[1:]:
            value = jnp.where(micro == 1, group[index][...], value)
        return value

    joined, inverse, gate = pick(1), pick(3), pick(4)
    inner = out_ref.shape[1]
    gate_part, up_part = joined[:, :inner], joined[:, inner:]
    sigmoid_gate = jax.nn.sigmoid(gate_part)
    silu_gate = gate_part * sigmoid_gate
    scaled_grad = (gate.astype(bf16).astype(f32) * upstream_f).astype(bf16)
    scaled_grad_ref[...] = scaled_grad
    act_grad = jnp.dot(scaled_grad, out_ref[...], preferred_element_type=f32)
    gate_grad = act_grad * up_part * sigmoid_gate * (1.0 + gate_part * (1.0 - sigmoid_gate))
    up_grad = act_grad * silu_gate
    joined_grad = jnp.concatenate([gate_grad, up_grad], axis=-1).astype(bf16)
    joined_grad_ref[...] = joined_grad
    if passes:
        rows_grad = jnp.dot(joined_grad, in_ref[...], preferred_element_type=f32).astype(bf16)
        share_grad = jnp.sum(pick(2).astype(f32) * upstream_f, axis=-1, keepdims=True)
        logit_grad = share_grad.astype(bf16).astype(f32) * gate * (1.0 - gate)
        gained = (rows_grad.astype(f32) + logit_grad * column_ref[...]) * gain_ref[...].astype(f32)
        scaled = pick(0).astype(f32) * inverse
        centred = gained - scaled * jnp.mean(gained * scaled, axis=-1, keepdims=True)
        passed = (upstream_f + inverse * centred).astype(bf16)
        split_rows(sent, passed, layer == last, ahead)


def record_kernel(plan, place_ref, *refs):
    layers, micros, sets, aliased = plan
    refs = list(refs)
    take = lambda number: [refs.pop(0) for _ in range(number)]
    grads = take(2)
    saved = [take(2) for _ in range(sets)]
    take(4 * aliased)
    kept = take(4)
    sems = refs.pop(0)
    micro = place_ref[2] - (2 * (layers - 1) - place_ref[0])
    slot = jnp.where((micro >= 0) & (micro < micros), micro, micros)

    def copy_all(chosen):
        sources = (chosen[0], grads[0], chosen[1], grads[1])
        copies = [
            pltpu.make_async_copy(sources[i], kept[i].at[slot], sems.at[i]) for i in range(4)
        ]
        for copy in copies:
            copy.start()
        for copy in copies:
            copy.wait()

    if sets == 1:
        copy_all(saved[0])
    else:
        pl.when(micro != 1)(lambda: copy_all(saved[0]))
        pl.when(micro == 1)(lambda: copy_all(saved[1]))


def resort_kernel(plan, place_ref, order_ref, *refs):
    arrivals, count, width, entry, last = plan
    arrived = refs[:arrivals]
    rest = refs[arrivals:]
    sent = rest[-count:]
    value = jnp.dot(
        order_ref[0], joined_rows(arrived, width), preferred_element_type=f32
    ).astype(bf16)
    if entry:
        layer = place_ref[0]
        value = jnp.where((layer == 0) | (layer == last), rest[0][...], value)
    split_rows(sent, value)


def prepare_kernel(plan, place_ref, *refs):
    homes, layers, micros, ranks, room, size, count = plan
    routes, entering = refs[:homes], refs[homes : 2 * homes]
    sent = refs[2 * homes : 2 * homes + count]
    start_ref, order_ref = refs[2 * homes + count :]
    layer, rank = place_ref[0], place_ref[1]
    tokens = routes[0].shape[1]
    rows = size * count
    near = [jnp.maximum(layer - 1, 0), layer, jnp.minimum(layer + 1, layers - 1)]
    ids = [
        [[routes[j][pl.ds(at * micros + m, 1), :] for m in range(micros)] for at in near]
        for j in range(homes)
    ]
    experts = lax.broadcasted_iota(jnp.int32, (ranks, tokens), 0)
    before = (
        lax.broadcasted_iota(jnp.int32, (tokens, tokens), 0)
        < lax.broadcasted_iota(jnp.int32, (tokens, tokens), 1)
    ).astype(f32).astype(bf16)
    flat = [row for home in ids for at in home for row in at]
    marks = jnp.concatenate([(experts == row).astype(f32) for row in flat], axis=0)
    earlier = marks * jnp.dot(marks.astype(bf16), before, preferred_element_type=f32)
    within = [
        jnp.sum(earlier[i * ranks : (i + 1) * ranks], axis=0, keepdims=True).astype(jnp.int32)
        for i in range(len(flat))
    ]

    def one_hot(size, index):
        slots = lax.broadcasted_iota(jnp.int32, (size, tokens), 0)
        return (slots == index).astype(f32).astype(bf16)

    def places(j, at, m):
        row, depth = ids[j][at][m], within[(j * 3 + at) * micros + m]
        if homes == 1:
            index = row * room + depth
            return index, index
        offset = row ^ rank
        far, other = offset >> 1, offset & 1
        target = jnp.where(other == 0, far * size + j * room + depth, -1)
        side = other if j == 0 else 1 - other
        return target, other * rows + far * size + side * room + depth

    for m in range(micros):
        here = [one_hot(rows, places(j, 1, m)[0]) for j in range(homes)]
        for which, at in enumerate((0, 2)):
            total = 0.0
            for j in range(homes):
                there = one_hot(homes * rows, places(j, at, m)[1])
                total += lax.dot_general(here[j], there, LAST, preferred_element_type=f32)
            order_ref[which * micros + m] = total.astype(bf16)
        start = 0.0
        for j in range(homes):
            start += jnp.dot(here[j], entering[j][m], preferred_element_type=f32)
        if m == 0:
            split_rows(sent, start.astype(bf16))
        else:
            start_ref[m - 1] = start.astype(bf16)


def fetch_kernel(in_ref, out_ref, in_near, out_near, sems):
    copies = [
        pltpu.make_async_copy(in_ref, in_near, sems.at[0]),
        pltpu.make_async_copy(out_ref, out_near, sems.at[1]),
    ]
    for copy in copies:
        copy.start()
    for copy in copies:
        copy.wait()


def transpose_kernel(in_ref, out_ref, in_turned, out_turned):
    in_turned[...] = in_ref[...].T
    out_turned[...] = out_ref[...].T


def grads_kernel(parts, place_ref, *refs):
    in_ref, out_ref = refs[8 * parts :]
    first = place_ref[0] == 0

    def gathered(which):
        blocks = []
        for part in range(parts):
            ref = refs[8 * part + which]
            micros = ref.shape[0]
            for m in range(micros):
                block = ref[m]
                if m == micros - 1:
                    block = jnp.where(first, refs[8 * part + which + 4][...], block)
                blocks.append(block)
        return jnp.concatenate(blocks, axis=0)

    in_ref[...] = lax.dot_general(
        gathered(0), gathered(1), FIRST, preferred_element_type=f32
    ).astype(bf16)
    out_ref[...] = lax.dot_general(
        gathered(2), gathered(3), FIRST, preferred_element_type=f32
    ).astype(bf16)


def shards(tokens_in, out_grad, routes, router, norm_gain, w_in, w_out):
    layers = lax.axis_size("pipe")
    ranks = lax.axis_size("expert")
    layer = lax.axis_index("pipe")
    rank = lax.axis_index("expert")
    micros, tokens, width = tokens_in.shape
    assert routes.shape[3] == 1 and router.shape[2] == ranks
    assert micros == 2 and layers > 2 and layers % 2 == 0
    capacity = max(2, tokens * 3 // (2 * ranks))
    paired = ranks <= WIDEST and ranks & (ranks - 1) == 0 and capacity >= 8
    count = ranks // 2 if paired else 1
    homes = 2 if paired else 1
    if paired:
        room = capacity
        size = -(-2 * room // 16) * 16
    else:
        room = -(-capacity // 4) * 4
        size = ranks * room
    rows = size * count
    tight = paired and size == 2 * room + 2 and width == LANES * (room + 1)
    short = width - LANES if tight else width
    parts = [[0, 3], [1, 2]] if count == 4 else [list(range(count))]
    last = layers - 1
    steps = 2 * last + micros
    own_in, own_out, gain_row = w_in[0, 0], w_out[0, 0], norm_gain
    double, inner = own_in.shape[1], own_out.shape[0]
    column = (
        lax.dynamic_index_in_dim(router[0], rank, 1, keepdims=False).astype(f32).reshape(1, width)
    )
    places = [
        jnp.stack([layer, rank, jnp.int32(step)]).astype(jnp.int32) for step in range(steps)
    ]
    piece = jax.ShapeDtypeStruct((size, short), bf16)
    params = pltpu.CompilerParams(vmem_limit_bytes=16 << 20)

    def permuted(block, offset, jump):
        route = []
        for p in range(layers):
            q = p if jump is None else jump(p)
            route += [(p * ranks + i, q * ranks + (i ^ offset)) for i in range(ranks)]
        return lax.ppermute(block, ("pipe", "expert"), route)

    def spread(pieces):
        return lax.all_to_all(
            pieces[0].reshape(ranks, room, width), "expert", split_axis=0, concat_axis=0, tiled=True
        ).reshape(rows, width)

    def to_experts(pieces):
        if not paired:
            return [spread(pieces)]
        arrived = [pieces[0]] + [None] * (count - 1)
        for k in sorted(range(1, count), key=lambda k: (k % 2, -k)):
            arrived[k] = permuted(pieces[k], 2 * k, None)
        return arrived

    def to_homes(pieces, jump):
        if not paired:
            return [lax.ppermute(spread(pieces), "pipe", [(p, jump(p)) for p in range(layers)])]
        arrived, swapped = [None] * count, [None] * count
        for part in parts:
            for k in reversed(part):
                arrived[k] = permuted(pieces[k], 2 * k, jump)
                swapped[k] = permuted(arrived[k], 1, None)
        return arrived + swapped

    entering = jnp.where(layer == 0, tokens_in, out_grad)
    ids = routes.reshape(layers * micros, tokens)
    both_ids, both_entering = [ids], [entering]
    if paired:
        both_ids.append(permuted(ids, 1, None))
        both_entering.append(permuted(entering, 1, None))
    *pieces, start, order = pl.pallas_call(
        functools.partial(prepare_kernel, (homes, layers, micros, ranks, room, size, count)),
        out_shape=[piece] * count
        + [
            jax.ShapeDtypeStruct((micros - 1, rows, width), bf16),
            jax.ShapeDtypeStruct((2 * micros, rows, homes * rows), bf16),
        ],
        in_specs=[SMEM] + [VMEM] * (2 * homes),
        out_specs=[VMEM] * (count + 2),
        compiler_params=params,
        name="prepare",
    )(places[0], *both_ids, *both_entering)

    def resort(step, arrived):
        def which(ref):
            forward_micro = ref[2] - ref[0]
            backward_micro = jnp.clip(forward_micro - 2 * (last - ref[0]), 0, micros - 1)
            is_forward = (forward_micro >= 0) & (forward_micro < micros)
            return jnp.where(is_forward, forward_micro, micros + backward_micro)

        entry = step < micros
        whole = lambda shape: pl.BlockSpec(shape, lambda i, ref: (0,) * len(shape))
        ins = list(arrived) + ([start[step - 1]] if entry else [])
        return pl.pallas_call(
            functools.partial(resort_kernel, (len(arrived), count, width, entry, last)),
            out_shape=[piece] * count,
            grid_spec=pltpu.PrefetchScalarGridSpec(
                num_scalar_prefetch=1,
                grid=(1,),
                in_specs=[
                    pl.BlockSpec((1, rows, homes * rows), lambda i, ref: (which(ref), 0, 0))
                ]
                + [whole(value.shape) for value in ins],
                out_specs=[whole((size, short))] * count,
            ),
            compiler_params=params,
            name="resort",
        )(places[step], order, *ins)

    own_in, own_out = pl.pallas_call(
        fetch_kernel,
        out_shape=[
            jax.ShapeDtypeStruct(own_in.shape, bf16),
            jax.ShapeDtypeStruct(own_out.shape, bf16),
        ],
        in_specs=[ANY] * 2,
        out_specs=[VMEM] * 2,
        scratch_shapes=[pltpu.SemaphoreType.DMA((2,))],
        compiler_params=params,
        name="fetch",
    )(own_in, own_out)

    def forward(arrived, earlier):
        many = len(arrived)
        form = lambda length, dtype: jax.ShapeDtypeStruct((many * size, length), dtype)
        out = pl.pallas_call(
            functools.partial(forward_kernel, many, len(earlier)),
            out_shape=[piece] * many
            + [
                form(width, bf16),
                form(double, f32),
                form(width, bf16),
                form(1, f32),
                form(1, f32),
                form(width, bf16),
                form(inner, bf16),
            ],
            in_specs=[VMEM] * (4 + many) + [ANY] * len(earlier),
            out_specs=[VMEM] * (many + 7),
            compiler_params=params,
            name="forward",
        )(gain_row, column, own_in, own_out, *arrived, *earlier)
        return out[:many], out[many:]

    def record(step, grads, saved, kept):
        sources = sources_of(step, saved)
        operands = [places[step], *grads]
        for group in sources:
            operands += group[5:]
        specs = [SMEM] + [ANY] * (len(operands) - 1)
        aliases = {}
        if kept is not None:
            aliases = {len(operands) + i: i for i in range(4)}
            operands += kept
            specs += [ANY] * 4
        depth = grads[0].shape[0]
        return pl.pallas_call(
            functools.partial(record_kernel, (layers, micros, len(sources), kept is not None)),
            out_shape=[
                jax.ShapeDtypeStruct((micros + 1, depth, length), bf16)
                for length in (width, double, inner, width)
            ],
            in_specs=specs,
            out_specs=[ANY] * 4,
            scratch_shapes=[pltpu.SemaphoreType.DMA((4,))],
            input_output_aliases=aliases,
            compiler_params=params,
            name="record",
        )(*operands)

    def sources_of(step, saved):
        return [
            saved[step - 2 * (last - p)]
            for p in range(layers)
            if 0 <= step - (2 * last - p) < micros
        ]

    bands = 8
    turned_in, turned_out = pl.pallas_call(
        transpose_kernel,
        grid=(bands,),
        out_shape=[
            jax.ShapeDtypeStruct((double, width), bf16),
            jax.ShapeDtypeStruct((width, inner), bf16),
        ],
        in_specs=[
            pl.BlockSpec((width // bands, double), lambda i: (i, 0)),
            pl.BlockSpec((inner, width // bands), lambda i: (0, i)),
        ],
        out_specs=[
            pl.BlockSpec((double, width // bands), lambda i: (0, i)),
            pl.BlockSpec((width // bands, inner), lambda i: (i, 0)),
        ],
        compiler_params=params,
        name="turn",
    )(own_in, own_out)

    def backward(step, arrived, entered, ahead, saved, earlier):
        passes = step + 1 < steps
        many = len(arrived)
        sources = sources_of(step, saved)
        plan = (
            many,
            layers,
            micros,
            len(sources),
            entered is not None,
            step == last,
            len(earlier),
            passes,
        )
        operands = [places[step], gain_row, column, turned_in, turned_out, *arrived]
        if entered is not None:
            operands += entered
        if step == last:
            operands += ahead
        for group in sources:
            operands += group[:5]
        specs = [SMEM] + [VMEM] * (len(operands) - 1) + [ANY] * len(earlier)
        operands += earlier
        sent = many if passes else 0
        out = pl.pallas_call(
            functools.partial(backward_kernel, plan),
            out_shape=[piece] * sent
            + [
                jax.ShapeDtypeStruct((many * size, length), bf16) for length in (double, width)
            ],
            in_specs=specs,
            out_specs=[VMEM] * (sent + 2),
            compiler_params=params,
            name="backward",
        )(*operands)
        return out[:sent], out[sent:]

    arrivals = []
    forwards = [[] for _ in parts]
    kept = [None for _ in parts]
    grads = [None for _ in parts]
    for step in range(steps):
        arrived = to_experts(pieces)
        arrivals.append(arrived)
        pieces, earlier = [None] * count, []
        for index, part in enumerate(parts):
            here = [arrived[k] for k in part]
            passed = None
            if step < last + micros:
                passed, saved = forward(here, earlier)
                forwards[index].append(saved)
            if step >= last:
                entered = None
                if step < last + micros:
                    entered = [arrivals[step - last][k] for k in part]
                passed, grads[index] = backward(
                    step, here, entered, passed, forwards[index], earlier
                )
                if step + 1 < steps:
                    kept[index] = record(
                        step, grads[index], forwards[index], kept[index]
                    )
            for k, value in zip(part, passed):
                pieces[k] = value
            earlier = passed[:1]
        if step + 1 == steps:
            break
        if step < last:
            jump = lambda p: (p + 1) % layers
        elif step == last:
            jump = lambda p: p ^ 1
        else:
            jump = lambda p: (p - 1) % layers
        pieces = resort(step + 1, to_homes(pieces, jump))

    cuts = 4
    specs = []
    for part in parts:
        depth = len(part) * size
        column_block = lambda length: pl.BlockSpec((micros, depth, length), lambda i: (0, 0, i))
        whole_block = lambda length: pl.BlockSpec((micros, depth, length), lambda i: (0, 0, 0))
        specs += [
            column_block(width // cuts),
            whole_block(double),
            column_block(inner // cuts),
            whole_block(width),
            pl.BlockSpec((depth, width // cuts), lambda i: (0, i)),
            pl.BlockSpec((depth, double), lambda i: (0, 0)),
            pl.BlockSpec((depth, inner // cuts), lambda i: (0, i)),
            pl.BlockSpec((depth, width), lambda i: (0, 0)),
        ]
    final = []
    for group, pair, saved in zip(kept, grads, forwards):
        normed, activated = saved[steps - 1 - 2 * last][5:]
        final += [*group, normed, pair[0], activated, pair[1]]
    grad_in, grad_out = pl.pallas_call(
        functools.partial(grads_kernel, len(parts)),
        grid=(cuts,),
        out_shape=[
            jax.ShapeDtypeStruct((width, double), bf16),
            jax.ShapeDtypeStruct((inner, width), bf16),
        ],
        in_specs=[SMEM] + specs,
        out_specs=[
            pl.BlockSpec((width // cuts, double), lambda i: (i, 0)),
            pl.BlockSpec((inner // cuts, width), lambda i: (i, 0)),
        ],
        compiler_params=params,
        name="grads",
    )(places[0], *final)
    return grad_in[None, None], grad_out[None, None]


def solution(mesh):
    placed = (
        P(None, "expert", None),
        P(None, "expert", None),
        P(None, None, "expert", None),
        P("pipe", None, None),
        P("pipe", None),
        P("pipe", "expert", None, None),
        P("pipe", "expert", None, None),
    )
    return jax.shard_map(
        shards,
        mesh=mesh,
        in_specs=placed,
        out_specs=(P("pipe", "expert", None, None), P("pipe", "expert", None, None)),
        check_vma=False,
    )
```

```python
import functools

import jax
import jax.numpy as jnp
from jax import lax
from jax.experimental import pallas as pl
from jax.experimental.pallas import tpu as pltpu
from jax.sharding import PartitionSpec as P


epsilon = 1e-06


f32, bf16 = jnp.float32, jnp.bfloat16
VMEM = pl.BlockSpec(memory_space=pltpu.VMEM)
SMEM = pl.BlockSpec(memory_space=pltpu.SMEM)
ANY = pl.BlockSpec(memory_space=pl.ANY)
LAST = (((1,), (1,)), ((), ()))
FIRST = (((0,), (0,)), ((), ()))
LANES = 128
WIDEST = 8


def unpacked(ref, width):
    value = ref[...]
    size = value.shape[0]
    if value.shape[1] == width:
        return value
    real = size - 2
    spare = value[real:].astype(f32)
    blocks = [spare[:, i * LANES : (i + 1) * LANES] for i in range(real // 2)]
    tail = jnp.concatenate(blocks + [jnp.zeros((2, LANES), f32)], axis=0).astype(bf16)
    held = lax.broadcasted_iota(jnp.int32, value.shape, 0) < real
    return jnp.concatenate([jnp.where(held, value, jnp.zeros_like(value)), tail], axis=1)


def packed(value, short):
    if value.shape[1] == short:
        return value
    real = value.shape[0] - 2
    tail = value[:, short:].astype(f32)
    spare = jnp.concatenate([tail[2 * i : 2 * i + 2] for i in range(real // 2)], axis=1)
    last = value[-16:, :short].astype(f32)
    last = jnp.concatenate([last[:14], spare], axis=0).astype(bf16)
    return jnp.concatenate([value[:-16, :short], last], axis=0)


def joined_rows(refs, width):
    parts = [unpacked(ref, width) for ref in refs]
    return parts[0] if len(parts) == 1 else jnp.concatenate(parts, axis=0)


def split_rows(refs, value, keep=None, others=None):
    size, short = refs[0].shape
    for k, ref in enumerate(refs):
        block = packed(value[k * size : (k + 1) * size], short)
        if others is not None:
            block = jnp.where(keep, block, others[k][...])
        ref[...] = block


def normalize(hidden, gain):
    values = hidden.astype(f32)
    inverse = lax.rsqrt(jnp.mean(values * values, axis=-1, keepdims=True) + epsilon)
    scaled = values * inverse
    return (scaled * gain).astype(bf16), scaled, inverse


def gate_of(normed, column):
    return jax.nn.sigmoid(jnp.sum(normed.astype(f32) * column, axis=-1, keepdims=True))


def forward_kernel(count, chained, passes, gain_ref, column_ref, in_ref, out_ref, *refs):
    arrived, refs = refs[:count], refs[count + chained :]
    if passes:
        sent, refs = refs[:count], refs[count:]
    hidden_ref, joined_ref, produced_ref, inverse_ref, gate_ref, normed_ref, activated_ref = refs
    inner = out_ref.shape[0]
    hidden = joined_rows(arrived, in_ref.shape[0])
    normed, _, inverse = normalize(hidden, gain_ref[...].astype(f32))
    gate = gate_of(normed, column_ref[...])
    share = gate.astype(bf16).astype(f32)
    joined = jnp.dot(normed, in_ref[...], preferred_element_type=f32)
    gate_part = joined[:, :inner]
    activated = (gate_part * jax.nn.sigmoid(gate_part) * joined[:, inner:]).astype(bf16)
    produced = jnp.dot(activated, out_ref[...], preferred_element_type=f32).astype(bf16)
    if passes:
        output = (hidden.astype(f32) + share * produced.astype(f32)).astype(bf16)
        split_rows(sent, output)
    hidden_ref[...] = hidden
    joined_ref[...] = joined
    produced_ref[...] = produced
    inverse_ref[...] = inverse
    gate_ref[...] = gate
    normed_ref[...] = normed
    activated_ref[...] = activated


def backward_kernel(plan, place_ref, gain_ref, column_ref, in_ref, out_ref, *refs):
    count, layers, _, sets, enters, first, chained, passes = plan
    last = layers - 1
    layer, step = place_ref[0], place_ref[2]
    refs = list(refs)
    take = lambda number: [refs.pop(0) for _ in range(number)]
    arrived = take(count)
    entered = take(count) if enters else None
    ahead = take(count) if first else None
    saved = [take(5) for _ in range(sets)]
    take(chained)
    sent = take(count) if passes else None
    joined_grad_ref, scaled_grad_ref = refs
    width = out_ref.shape[0]
    upstream = joined_rows(arrived, width)
    if entered is not None:
        upstream = jnp.where(layer == last, joined_rows(entered, width), upstream)
    upstream_f = upstream.astype(f32)
    micro = step - (2 * last - layer)

    def pick(index):
        value = saved[0][index][...]
        for group in saved[1:]:
            value = jnp.where(micro == 1, group[index][...], value)
        return value

    joined, inverse, gate = pick(1), pick(3), pick(4)
    inner = out_ref.shape[1]
    gate_part, up_part = joined[:, :inner], joined[:, inner:]
    sigmoid_gate = jax.nn.sigmoid(gate_part)
    silu_gate = gate_part * sigmoid_gate
    scaled_grad = (gate.astype(bf16).astype(f32) * upstream_f).astype(bf16)
    scaled_grad_ref[...] = scaled_grad
    act_grad = jnp.dot(scaled_grad, out_ref[...], preferred_element_type=f32)
    gate_grad = act_grad * up_part * sigmoid_gate * (1.0 + gate_part * (1.0 - sigmoid_gate))
    up_grad = act_grad * silu_gate
    joined_grad = jnp.concatenate([gate_grad, up_grad], axis=-1).astype(bf16)
    joined_grad_ref[...] = joined_grad
    if passes:
        rows_grad = jnp.dot(joined_grad, in_ref[...], preferred_element_type=f32).astype(bf16)
        share_grad = jnp.sum(pick(2).astype(f32) * upstream_f, axis=-1, keepdims=True)
        logit_grad = share_grad.astype(bf16).astype(f32) * gate * (1.0 - gate)
        gained = (rows_grad.astype(f32) + logit_grad * column_ref[...]) * gain_ref[...].astype(f32)
        scaled = pick(0).astype(f32) * inverse
        centred = gained - scaled * jnp.mean(gained * scaled, axis=-1, keepdims=True)
        passed = (upstream_f + inverse * centred).astype(bf16)
        split_rows(sent, passed, layer == last, ahead)


def record_kernel(plan, place_ref, *refs):
    layers, micros, sets, aliased = plan
    refs = list(refs)
    take = lambda number: [refs.pop(0) for _ in range(number)]
    grads = take(2)
    saved = [take(2) for _ in range(sets)]
    take(4 * aliased)
    kept = take(4)
    sems = refs.pop(0)
    micro = place_ref[2] - (2 * (layers - 1) - place_ref[0])
    slot = jnp.where((micro >= 0) & (micro < micros), micro, micros)

    def copy_all(chosen):
        sources = (chosen[0], grads[0], chosen[1], grads[1])
        copies = [
            pltpu.make_async_copy(sources[i], kept[i].at[slot], sems.at[i]) for i in range(4)
        ]
        for copy in copies:
            copy.start()
        for copy in copies:
            copy.wait()

    if sets == 1:
        copy_all(saved[0])
    else:
        pl.when(micro != 1)(lambda: copy_all(saved[0]))
        pl.when(micro == 1)(lambda: copy_all(saved[1]))


def resort_kernel(plan, place_ref, order_ref, *refs):
    arrivals, count, width, entry, last = plan
    arrived = refs[:arrivals]
    rest = refs[arrivals:]
    sent = rest[-count:]
    value = jnp.dot(
        order_ref[0], joined_rows(arrived, width), preferred_element_type=f32
    ).astype(bf16)
    if entry:
        layer = place_ref[0]
        value = jnp.where((layer == 0) | (layer == last), rest[0][...], value)
    split_rows(sent, value)


def prepare_kernel(plan, place_ref, *refs):
    homes, layers, micros, ranks, room, size, count = plan
    routes, entering = refs[:homes], refs[homes : 2 * homes]
    sent = refs[2 * homes : 2 * homes + count]
    start_ref, order_ref = refs[2 * homes + count :]
    layer, rank = place_ref[0], place_ref[1]
    tokens = routes[0].shape[1]
    rows = size * count
    near = [jnp.maximum(layer - 1, 0), layer, jnp.minimum(layer + 1, layers - 1)]
    ids = [
        [[routes[j][pl.ds(at * micros + m, 1), :] for m in range(micros)] for at in near]
        for j in range(homes)
    ]
    experts = lax.broadcasted_iota(jnp.int32, (ranks, tokens), 0)
    before = (
        lax.broadcasted_iota(jnp.int32, (tokens, tokens), 0)
        < lax.broadcasted_iota(jnp.int32, (tokens, tokens), 1)
    ).astype(f32).astype(bf16)
    flat = [row for home in ids for at in home for row in at]
    marks = jnp.concatenate([(experts == row).astype(f32) for row in flat], axis=0)
    earlier = marks * jnp.dot(marks.astype(bf16), before, preferred_element_type=f32)
    within = [
        jnp.sum(earlier[i * ranks : (i + 1) * ranks], axis=0, keepdims=True).astype(jnp.int32)
        for i in range(len(flat))
    ]

    def one_hot(size, index):
        slots = lax.broadcasted_iota(jnp.int32, (size, tokens), 0)
        return (slots == index).astype(f32).astype(bf16)

    def places(j, at, m):
        row, depth = ids[j][at][m], within[(j * 3 + at) * micros + m]
        if homes == 1:
            index = row * room + depth
            return index, index
        offset = row ^ rank
        far, other = offset >> 1, offset & 1
        target = jnp.where(other == 0, far * size + j * room + depth, -1)
        side = other if j == 0 else 1 - other
        return target, other * rows + far * size + side * room + depth

    for m in range(micros):
        here = [one_hot(rows, places(j, 1, m)[0]) for j in range(homes)]
        for which, at in enumerate((0, 2)):
            total = 0.0
            for j in range(homes):
                there = one_hot(homes * rows, places(j, at, m)[1])
                total += lax.dot_general(here[j], there, LAST, preferred_element_type=f32)
            order_ref[which * micros + m] = total.astype(bf16)
        start = 0.0
        for j in range(homes):
            start += jnp.dot(here[j], entering[j][m], preferred_element_type=f32)
        if m == 0:
            split_rows(sent, start.astype(bf16))
        else:
            start_ref[m - 1] = start.astype(bf16)


def fetch_kernel(in_ref, out_ref, in_near, out_near, sems):
    copies = [
        pltpu.make_async_copy(in_ref, in_near, sems.at[0]),
        pltpu.make_async_copy(out_ref, out_near, sems.at[1]),
    ]
    for copy in copies:
        copy.start()
    for copy in copies:
        copy.wait()


def transpose_kernel(in_ref, out_ref, in_turned, out_turned):
    in_turned[...] = in_ref[...].T
    out_turned[...] = out_ref[...].T


def grads_kernel(parts, place_ref, *refs):
    in_ref, out_ref = refs[8 * parts :]
    first = place_ref[0] == 0

    def gathered(which):
        blocks = []
        for part in range(parts):
            ref = refs[8 * part + which]
            micros = ref.shape[0]
            for m in range(micros):
                block = ref[m]
                if m == micros - 1:
                    block = jnp.where(first, refs[8 * part + which + 4][...], block)
                blocks.append(block)
        return jnp.concatenate(blocks, axis=0)

    in_ref[...] = lax.dot_general(
        gathered(0), gathered(1), FIRST, preferred_element_type=f32
    ).astype(bf16)
    out_ref[...] = lax.dot_general(
        gathered(2), gathered(3), FIRST, preferred_element_type=f32
    ).astype(bf16)


def shards(tokens_in, out_grad, routes, router, norm_gain, w_in, w_out):
    layers = lax.axis_size("pipe")
    ranks = lax.axis_size("expert")
    layer = lax.axis_index("pipe")
    rank = lax.axis_index("expert")
    micros, tokens, width = tokens_in.shape
    assert routes.shape[3] == 1 and router.shape[2] == ranks
    assert micros == 2 and layers > 2 and layers % 2 == 0
    capacity = max(2, tokens * 3 // (2 * ranks))
    paired = ranks <= WIDEST and ranks & (ranks - 1) == 0 and capacity >= 8
    count = ranks // 2 if paired else 1
    homes = 2 if paired else 1
    if paired:
        room = capacity
        size = -(-2 * room // 16) * 16
    else:
        room = -(-capacity // 4) * 4
        size = ranks * room
    rows = size * count
    tight = paired and size == 2 * room + 2 and width == LANES * (room + 1)
    short = width - LANES if tight else width
    parts = [[0, 3], [1, 2]] if count == 4 else [list(range(count))]
    last = layers - 1
    steps = 2 * last + micros
    own_in, own_out, gain_row = w_in[0, 0], w_out[0, 0], norm_gain
    double, inner = own_in.shape[1], own_out.shape[0]
    column = (
        lax.dynamic_index_in_dim(router[0], rank, 1, keepdims=False).astype(f32).reshape(1, width)
    )
    places = [
        jnp.stack([layer, rank, jnp.int32(step)]).astype(jnp.int32) for step in range(steps)
    ]
    piece = jax.ShapeDtypeStruct((size, short), bf16)
    params = pltpu.CompilerParams(vmem_limit_bytes=16 << 20)

    def permuted(block, offset, jump):
        route = []
        for p in range(layers):
            q = p if jump is None else jump(p)
            route += [(p * ranks + i, q * ranks + (i ^ offset)) for i in range(ranks)]
        return lax.ppermute(block, ("pipe", "expert"), route)

    def spread(pieces):
        return lax.all_to_all(
            pieces[0].reshape(ranks, room, width), "expert", split_axis=0, concat_axis=0, tiled=True
        ).reshape(rows, width)

    def to_experts(pieces):
        if not paired:
            return [spread(pieces)]
        arrived = [pieces[0]] + [None] * (count - 1)
        for k in sorted(range(1, count), key=lambda k: (k % 2, -k)):
            arrived[k] = permuted(pieces[k], 2 * k, None)
        return arrived

    def to_homes(pieces, jump):
        if not paired:
            return [lax.ppermute(spread(pieces), "pipe", [(p, jump(p)) for p in range(layers)])]
        arrived, swapped = [None] * count, [None] * count
        for part in parts:
            for k in reversed(part):
                arrived[k] = permuted(pieces[k], 2 * k, jump)
                swapped[k] = permuted(arrived[k], 1, None)
        return arrived + swapped

    entering = jnp.where(layer == 0, tokens_in, out_grad)
    ids = routes.reshape(layers * micros, tokens)
    both_ids, both_entering = [ids], [entering]
    if paired:
        both_ids.append(permuted(ids, 1, None))
        both_entering.append(permuted(entering, 1, None))
    *pieces, start, order = pl.pallas_call(
        functools.partial(prepare_kernel, (homes, layers, micros, ranks, room, size, count)),
        out_shape=[piece] * count
        + [
            jax.ShapeDtypeStruct((micros - 1, rows, width), bf16),
            jax.ShapeDtypeStruct((2 * micros, rows, homes * rows), bf16),
        ],
        in_specs=[SMEM] + [VMEM] * (2 * homes),
        out_specs=[VMEM] * (count + 2),
        compiler_params=params,
        name="prepare",
    )(places[0], *both_ids, *both_entering)

    def resort(step, arrived):
        def which(ref):
            forward_micro = ref[2] - ref[0]
            backward_micro = jnp.clip(forward_micro - 2 * (last - ref[0]), 0, micros - 1)
            is_forward = (forward_micro >= 0) & (forward_micro < micros)
            return jnp.where(is_forward, forward_micro, micros + backward_micro)

        entry = step < micros
        whole = lambda shape: pl.BlockSpec(shape, lambda i, ref: (0,) * len(shape))
        ins = list(arrived) + ([start[step - 1]] if entry else [])
        return pl.pallas_call(
            functools.partial(resort_kernel, (len(arrived), count, width, entry, last)),
            out_shape=[piece] * count,
            grid_spec=pltpu.PrefetchScalarGridSpec(
                num_scalar_prefetch=1,
                grid=(1,),
                in_specs=[
                    pl.BlockSpec((1, rows, homes * rows), lambda i, ref: (which(ref), 0, 0))
                ]
                + [whole(value.shape) for value in ins],
                out_specs=[whole((size, short))] * count,
            ),
            compiler_params=params,
            name="resort",
        )(places[step], order, *ins)

    own_in, own_out = pl.pallas_call(
        fetch_kernel,
        out_shape=[
            jax.ShapeDtypeStruct(own_in.shape, bf16),
            jax.ShapeDtypeStruct(own_out.shape, bf16),
        ],
        in_specs=[ANY] * 2,
        out_specs=[VMEM] * 2,
        scratch_shapes=[pltpu.SemaphoreType.DMA((2,))],
        compiler_params=params,
        name="fetch",
    )(own_in, own_out)

    def forward(step, arrived, earlier):
        many = len(arrived)
        passes = step <= last
        sent = many if passes else 0
        form = lambda length, dtype: jax.ShapeDtypeStruct((many * size, length), dtype)
        out = pl.pallas_call(
            functools.partial(forward_kernel, many, len(earlier), passes),
            out_shape=[piece] * sent
            + [
                form(width, bf16),
                form(double, f32),
                form(width, bf16),
                form(1, f32),
                form(1, f32),
                form(width, bf16),
                form(inner, bf16),
            ],
            in_specs=[VMEM] * (4 + many) + [ANY] * len(earlier),
            out_specs=[VMEM] * (sent + 7),
            compiler_params=params,
            name="forward",
        )(gain_row, column, own_in, own_out, *arrived, *earlier)
        return out[:sent], out[sent:]

    def record(step, grads, saved, kept):
        sources = sources_of(step, saved)
        operands = [places[step], *grads]
        for group in sources:
            operands += group[5:]
        specs = [SMEM] + [ANY] * (len(operands) - 1)
        aliases = {}
        if kept is not None:
            aliases = {len(operands) + i: i for i in range(4)}
            operands += kept
            specs += [ANY] * 4
        depth = grads[0].shape[0]
        return pl.pallas_call(
            functools.partial(record_kernel, (layers, micros, len(sources), kept is not None)),
            out_shape=[
                jax.ShapeDtypeStruct((micros + 1, depth, length), bf16)
                for length in (width, double, inner, width)
            ],
            in_specs=specs,
            out_specs=[ANY] * 4,
            scratch_shapes=[pltpu.SemaphoreType.DMA((4,))],
            input_output_aliases=aliases,
            compiler_params=params,
            name="record",
        )(*operands)

    def sources_of(step, saved):
        return [
            saved[step - 2 * (last - p)]
            for p in range(layers)
            if 0 <= step - (2 * last - p) < micros
        ]

    bands = 8
    turned_in, turned_out = pl.pallas_call(
        transpose_kernel,
        grid=(bands,),
        out_shape=[
            jax.ShapeDtypeStruct((double, width), bf16),
            jax.ShapeDtypeStruct((width, inner), bf16),
        ],
        in_specs=[
            pl.BlockSpec((width // bands, double), lambda i: (i, 0)),
            pl.BlockSpec((inner, width // bands), lambda i: (0, i)),
        ],
        out_specs=[
            pl.BlockSpec((double, width // bands), lambda i: (0, i)),
            pl.BlockSpec((width // bands, inner), lambda i: (i, 0)),
        ],
        compiler_params=params,
        name="turn",
    )(own_in, own_out)

    def backward(step, arrived, entered, ahead, saved, earlier):
        passes = step + 1 < steps
        many = len(arrived)
        sources = sources_of(step, saved)
        plan = (
            many,
            layers,
            micros,
            len(sources),
            entered is not None,
            step == last,
            len(earlier),
            passes,
        )
        operands = [places[step], gain_row, column, turned_in, turned_out, *arrived]
        if entered is not None:
            operands += entered
        if step == last:
            operands += ahead
        for group in sources:
            operands += group[:5]
        specs = [SMEM] + [VMEM] * (len(operands) - 1) + [ANY] * len(earlier)
        operands += earlier
        sent = many if passes else 0
        out = pl.pallas_call(
            functools.partial(backward_kernel, plan),
            out_shape=[piece] * sent
            + [
                jax.ShapeDtypeStruct((many * size, length), bf16) for length in (double, width)
            ],
            in_specs=specs,
            out_specs=[VMEM] * (sent + 2),
            compiler_params=params,
            name="backward",
        )(*operands)
        return out[:sent], out[sent:]

    arrivals = []
    forwards = [[] for _ in parts]
    kept = [None for _ in parts]
    grads = [None for _ in parts]
    for step in range(steps):
        arrived = to_experts(pieces)
        arrivals.append(arrived)
        pieces, earlier = [None] * count, []
        for index, part in enumerate(parts):
            here = [arrived[k] for k in part]
            passed = None
            if step < last + micros:
                passed, saved = forward(step, here, earlier)
                forwards[index].append(saved)
            if step >= last:
                entered = None
                if step < last + micros:
                    entered = [arrivals[step - last][k] for k in part]
                passed, grads[index] = backward(
                    step, here, entered, passed, forwards[index], earlier
                )
                if step + 1 < steps:
                    kept[index] = record(
                        step, grads[index], forwards[index], kept[index]
                    )
            for k, value in zip(part, passed):
                pieces[k] = value
            earlier = passed[:1]
        if step + 1 == steps:
            break
        if step < last:
            jump = lambda p: (p + 1) % layers
        elif step == last:
            jump = lambda p: p ^ 1
        else:
            jump = lambda p: (p - 1) % layers
        pieces = resort(step + 1, to_homes(pieces, jump))

    cuts = 4
    specs = []
    for part in parts:
        depth = len(part) * size
        column_block = lambda length: pl.BlockSpec((micros, depth, length), lambda i: (0, 0, i))
        whole_block = lambda length: pl.BlockSpec((micros, depth, length), lambda i: (0, 0, 0))
        specs += [
            column_block(width // cuts),
            whole_block(double),
            column_block(inner // cuts),
            whole_block(width),
            pl.BlockSpec((depth, width // cuts), lambda i: (0, i)),
            pl.BlockSpec((depth, double), lambda i: (0, 0)),
            pl.BlockSpec((depth, inner // cuts), lambda i: (0, i)),
            pl.BlockSpec((depth, width), lambda i: (0, 0)),
        ]
    final = []
    for group, pair, saved in zip(kept, grads, forwards):
        normed, activated = saved[steps - 1 - 2 * last][5:]
        final += [*group, normed, pair[0], activated, pair[1]]
    grad_in, grad_out = pl.pallas_call(
        functools.partial(grads_kernel, len(parts)),
        grid=(cuts,),
        out_shape=[
            jax.ShapeDtypeStruct((width, double), bf16),
            jax.ShapeDtypeStruct((inner, width), bf16),
        ],
        in_specs=[SMEM] + specs,
        out_specs=[
            pl.BlockSpec((width // cuts, double), lambda i: (i, 0)),
            pl.BlockSpec((inner // cuts, width), lambda i: (i, 0)),
        ],
        compiler_params=params,
        name="grads",
    )(places[0], *final)
    return grad_in[None, None], grad_out[None, None]


def solution(mesh):
    placed = (
        P(None, "expert", None),
        P(None, "expert", None),
        P(None, None, "expert", None),
        P("pipe", None, None),
        P("pipe", None),
        P("pipe", "expert", None, None),
        P("pipe", "expert", None, None),
    )
    return jax.shard_map(
        shards,
        mesh=mesh,
        in_specs=placed,
        out_specs=(P("pipe", "expert", None, None), P("pipe", "expert", None, None)),
        check_vma=False,
    )
```

```python
import functools

import jax
import jax.numpy as jnp
from jax import lax
from jax.experimental import pallas as pl
from jax.experimental.pallas import tpu as pltpu
from jax.sharding import PartitionSpec as P


epsilon = 1e-06


f32, bf16 = jnp.float32, jnp.bfloat16
VMEM = pl.BlockSpec(memory_space=pltpu.VMEM)
SMEM = pl.BlockSpec(memory_space=pltpu.SMEM)
ANY = pl.BlockSpec(memory_space=pl.ANY)
LAST = (((1,), (1,)), ((), ()))
FIRST = (((0,), (0,)), ((), ()))
LANES = 128
WIDEST = 8


def unpacked(ref, width):
    value = ref[...]
    size = value.shape[0]
    if value.shape[1] == width:
        return value
    real = size - 2
    spare = value[real:].astype(f32)
    blocks = [spare[:, i * LANES : (i + 1) * LANES] for i in range(real // 2)]
    tail = jnp.concatenate(blocks + [jnp.zeros((2, LANES), f32)], axis=0).astype(bf16)
    held = lax.broadcasted_iota(jnp.int32, value.shape, 0) < real
    return jnp.concatenate([jnp.where(held, value, jnp.zeros_like(value)), tail], axis=1)


def packed(value, short):
    if value.shape[1] == short:
        return value
    real = value.shape[0] - 2
    tail = value[:, short:].astype(f32)
    spare = jnp.concatenate([tail[2 * i : 2 * i + 2] for i in range(real // 2)], axis=1)
    last = value[-16:, :short].astype(f32)
    last = jnp.concatenate([last[:14], spare], axis=0).astype(bf16)
    return jnp.concatenate([value[:-16, :short], last], axis=0)


def joined_rows(refs, width):
    parts = [unpacked(ref, width) for ref in refs]
    return parts[0] if len(parts) == 1 else jnp.concatenate(parts, axis=0)


def split_rows(refs, value, keep=None, others=None):
    size, short = refs[0].shape
    for k, ref in enumerate(refs):
        block = packed(value[k * size : (k + 1) * size], short)
        if others is not None:
            block = jnp.where(keep, block, others[k][...])
        ref[...] = block


def normalize(hidden, gain):
    values = hidden.astype(f32)
    inverse = lax.rsqrt(jnp.mean(values * values, axis=-1, keepdims=True) + epsilon)
    scaled = values * inverse
    return (scaled * gain).astype(bf16), scaled, inverse


def gate_of(normed, column):
    return jax.nn.sigmoid(jnp.sum(normed.astype(f32) * column, axis=-1, keepdims=True))


def forward_kernel(count, chained, passes, gain_ref, column_ref, in_ref, out_ref, *refs):
    arrived, refs = refs[:count], refs[count + chained :]
    if passes:
        sent, refs = refs[:count], refs[count:]
    hidden_ref, joined_ref, produced_ref, inverse_ref, gate_ref, normed_ref, activated_ref = refs
    inner = out_ref.shape[0]
    hidden = joined_rows(arrived, in_ref.shape[0])
    normed, _, inverse = normalize(hidden, gain_ref[...].astype(f32))
    gate = gate_of(normed, column_ref[...])
    share = gate.astype(bf16).astype(f32)
    joined = jnp.dot(normed, in_ref[...], preferred_element_type=f32)
    gate_part = joined[:, :inner]
    activated = (gate_part * jax.nn.sigmoid(gate_part) * joined[:, inner:]).astype(bf16)
    produced = jnp.dot(activated, out_ref[...], preferred_element_type=f32).astype(bf16)
    if passes:
        output = (hidden.astype(f32) + share * produced.astype(f32)).astype(bf16)
        split_rows(sent, output)
    hidden_ref[...] = hidden
    joined_ref[...] = joined
    produced_ref[...] = produced
    inverse_ref[...] = inverse
    gate_ref[...] = gate
    normed_ref[...] = normed
    activated_ref[...] = activated


def backward_kernel(plan, place_ref, gain_ref, column_ref, in_ref, out_ref, *refs):
    count, layers, _, sets, enters, first, chained, passes = plan
    last = layers - 1
    layer, step = place_ref[0], place_ref[2]
    refs = list(refs)
    take = lambda number: [refs.pop(0) for _ in range(number)]
    arrived = take(count)
    entered = take(count) if enters else None
    ahead = take(count) if first else None
    saved = [take(5) for _ in range(sets)]
    take(chained)
    sent = take(count) if passes else None
    joined_grad_ref, scaled_grad_ref = refs
    width = out_ref.shape[0]
    upstream = joined_rows(arrived, width)
    if entered is not None:
        upstream = jnp.where(layer == last, joined_rows(entered, width), upstream)
    upstream_f = upstream.astype(f32)
    micro = step - (2 * last - layer)

    def pick(index):
        value = saved[0][index][...]
        for group in saved[1:]:
            value = jnp.where(micro == 1, group[index][...], value)
        return value

    joined, inverse, gate = pick(1), pick(3), pick(4)
    inner = out_ref.shape[1]
    gate_part, up_part = joined[:, :inner], joined[:, inner:]
    sigmoid_gate = jax.nn.sigmoid(gate_part)
    silu_gate = gate_part * sigmoid_gate
    scaled_grad = (gate.astype(bf16).astype(f32) * upstream_f).astype(bf16)
    scaled_grad_ref[...] = scaled_grad
    act_grad = jnp.dot(scaled_grad, out_ref[...], preferred_element_type=f32)
    gate_grad = act_grad * up_part * sigmoid_gate * (1.0 + gate_part * (1.0 - sigmoid_gate))
    up_grad = act_grad * silu_gate
    joined_grad = jnp.concatenate([gate_grad, up_grad], axis=-1).astype(bf16)
    joined_grad_ref[...] = joined_grad
    if passes:
        rows_grad = jnp.dot(joined_grad, in_ref[...], preferred_element_type=f32).astype(bf16)
        share_grad = jnp.sum(pick(2).astype(f32) * upstream_f, axis=-1, keepdims=True)
        logit_grad = share_grad.astype(bf16).astype(f32) * gate * (1.0 - gate)
        gained = (rows_grad.astype(f32) + logit_grad * column_ref[...]) * gain_ref[...].astype(f32)
        scaled = pick(0).astype(f32) * inverse
        centred = gained - scaled * jnp.mean(gained * scaled, axis=-1, keepdims=True)
        passed = (upstream_f + inverse * centred).astype(bf16)
        split_rows(sent, passed, layer == last, ahead)


def record_kernel(plan, place_ref, *refs):
    layers, micros, sets, aliased = plan
    refs = list(refs)
    take = lambda number: [refs.pop(0) for _ in range(number)]
    grads = take(2)
    saved = [take(2) for _ in range(sets)]
    take(4 * aliased)
    kept = take(4)
    sems = refs.pop(0)
    micro = place_ref[2] - (2 * (layers - 1) - place_ref[0])
    slot = jnp.where((micro >= 0) & (micro < micros), micro, micros)

    def copy_all(chosen):
        sources = (chosen[0], grads[0], chosen[1], grads[1])
        copies = [
            pltpu.make_async_copy(sources[i], kept[i].at[slot], sems.at[i]) for i in range(4)
        ]
        for copy in copies:
            copy.start()
        for copy in copies:
            copy.wait()

    if sets == 1:
        copy_all(saved[0])
    else:
        pl.when(micro != 1)(lambda: copy_all(saved[0]))
        pl.when(micro == 1)(lambda: copy_all(saved[1]))


def resort_kernel(plan, place_ref, order_ref, *refs):
    arrivals, count, width, micros, entry, last = plan
    arrived = refs[:arrivals]
    rest = refs[arrivals:]
    sent = rest[-count:]
    forward_micro = place_ref[2] - place_ref[0]
    backward_micro = jnp.clip(forward_micro - 2 * (last - place_ref[0]), 0, micros - 1)
    is_forward = (forward_micro >= 0) & (forward_micro < micros)
    which = jnp.where(is_forward, forward_micro, micros + backward_micro)
    value = jnp.dot(
        order_ref[which], joined_rows(arrived, width), preferred_element_type=f32
    ).astype(bf16)
    if entry:
        layer = place_ref[0]
        value = jnp.where((layer == 0) | (layer == last), rest[0][...], value)
    split_rows(sent, value)


def prepare_kernel(plan, place_ref, *refs):
    homes, layers, micros, ranks, room, size, count = plan
    routes, entering = refs[:homes], refs[homes : 2 * homes]
    sent = refs[2 * homes : 2 * homes + count]
    start_ref, order_ref = refs[2 * homes + count :]
    layer, rank = place_ref[0], place_ref[1]
    tokens = routes[0].shape[1]
    rows = size * count
    near = [jnp.maximum(layer - 1, 0), layer, jnp.minimum(layer + 1, layers - 1)]
    ids = [
        [[routes[j][pl.ds(at * micros + m, 1), :] for m in range(micros)] for at in near]
        for j in range(homes)
    ]
    experts = lax.broadcasted_iota(jnp.int32, (ranks, tokens), 0)
    before = (
        lax.broadcasted_iota(jnp.int32, (tokens, tokens), 0)
        < lax.broadcasted_iota(jnp.int32, (tokens, tokens), 1)
    ).astype(f32).astype(bf16)
    flat = [row for home in ids for at in home for row in at]
    marks = jnp.concatenate([(experts == row).astype(f32) for row in flat], axis=0)
    earlier = marks * jnp.dot(marks.astype(bf16), before, preferred_element_type=f32)
    within = [
        jnp.sum(earlier[i * ranks : (i + 1) * ranks], axis=0, keepdims=True).astype(jnp.int32)
        for i in range(len(flat))
    ]

    def one_hot(size, index):
        slots = lax.broadcasted_iota(jnp.int32, (size, tokens), 0)
        return (slots == index).astype(f32).astype(bf16)

    def places(j, at, m):
        row, depth = ids[j][at][m], within[(j * 3 + at) * micros + m]
        if homes == 1:
            index = row * room + depth
            return index, index
        offset = row ^ rank
        far, other = offset >> 1, offset & 1
        target = jnp.where(other == 0, far * size + j * room + depth, -1)
        side = other if j == 0 else 1 - other
        return target, other * rows + far * size + side * room + depth

    for m in range(micros):
        here = [one_hot(rows, places(j, 1, m)[0]) for j in range(homes)]
        for which, at in enumerate((0, 2)):
            total = 0.0
            for j in range(homes):
                there = one_hot(homes * rows, places(j, at, m)[1])
                total += lax.dot_general(here[j], there, LAST, preferred_element_type=f32)
            order_ref[which * micros + m] = total.astype(bf16)
        start = 0.0
        for j in range(homes):
            start += jnp.dot(here[j], entering[j][m], preferred_element_type=f32)
        if m == 0:
            split_rows(sent, start.astype(bf16))
        else:
            start_ref[m - 1] = start.astype(bf16)


def fetch_kernel(in_ref, out_ref, in_near, out_near, sems):
    copies = [
        pltpu.make_async_copy(in_ref, in_near, sems.at[0]),
        pltpu.make_async_copy(out_ref, out_near, sems.at[1]),
    ]
    for copy in copies:
        copy.start()
    for copy in copies:
        copy.wait()


def transpose_kernel(in_ref, out_ref, in_turned, out_turned):
    in_turned[...] = in_ref[...].T
    out_turned[...] = out_ref[...].T


def grads_kernel(parts, place_ref, *refs):
    in_ref, out_ref = refs[8 * parts :]
    first = place_ref[0] == 0

    def gathered(which):
        blocks = []
        for part in range(parts):
            ref = refs[8 * part + which]
            micros = ref.shape[0]
            for m in range(micros):
                block = ref[m]
                if m == micros - 1:
                    block = jnp.where(first, refs[8 * part + which + 4][...], block)
                blocks.append(block)
        return jnp.concatenate(blocks, axis=0)

    in_ref[...] = lax.dot_general(
        gathered(0), gathered(1), FIRST, preferred_element_type=f32
    ).astype(bf16)
    out_ref[...] = lax.dot_general(
        gathered(2), gathered(3), FIRST, preferred_element_type=f32
    ).astype(bf16)


def shards(tokens_in, out_grad, routes, router, norm_gain, w_in, w_out):
    layers = lax.axis_size("pipe")
    ranks = lax.axis_size("expert")
    layer = lax.axis_index("pipe")
    rank = lax.axis_index("expert")
    micros, tokens, width = tokens_in.shape
    assert routes.shape[3] == 1 and router.shape[2] == ranks
    assert micros == 2 and layers > 2 and layers % 2 == 0
    capacity = max(2, tokens * 3 // (2 * ranks))
    paired = ranks <= WIDEST and ranks & (ranks - 1) == 0 and capacity >= 8
    count = ranks // 2 if paired else 1
    homes = 2 if paired else 1
    if paired:
        room = capacity
        size = -(-2 * room // 16) * 16
    else:
        room = -(-capacity // 4) * 4
        size = ranks * room
    rows = size * count
    tight = paired and size == 2 * room + 2 and width == LANES * (room + 1)
    short = width - LANES if tight else width
    parts = [[0, 3], [1, 2]] if count == 4 else [list(range(count))]
    last = layers - 1
    steps = 2 * last + micros
    own_in, own_out, gain_row = w_in[0, 0], w_out[0, 0], norm_gain
    double, inner = own_in.shape[1], own_out.shape[0]
    column = (
        lax.dynamic_index_in_dim(router[0], rank, 1, keepdims=False).astype(f32).reshape(1, width)
    )
    places = [
        jnp.stack([layer, rank, jnp.int32(step)]).astype(jnp.int32) for step in range(steps)
    ]
    piece = jax.ShapeDtypeStruct((size, short), bf16)
    params = pltpu.CompilerParams(vmem_limit_bytes=16 << 20)

    def permuted(block, offset, jump):
        route = []
        for p in range(layers):
            q = p if jump is None else jump(p)
            route += [(p * ranks + i, q * ranks + (i ^ offset)) for i in range(ranks)]
        return lax.ppermute(block, ("pipe", "expert"), route)

    def spread(pieces):
        return lax.all_to_all(
            pieces[0].reshape(ranks, room, width), "expert", split_axis=0, concat_axis=0, tiled=True
        ).reshape(rows, width)

    def to_experts(pieces):
        if not paired:
            return [spread(pieces)]
        arrived = [pieces[0]] + [None] * (count - 1)
        for k in sorted(range(1, count), key=lambda k: (k % 2, -k)):
            arrived[k] = permuted(pieces[k], 2 * k, None)
        return arrived

    def to_homes(pieces, jump):
        if not paired:
            return [lax.ppermute(spread(pieces), "pipe", [(p, jump(p)) for p in range(layers)])]
        arrived, swapped = [None] * count, [None] * count
        for part in parts:
            for k in reversed(part):
                arrived[k] = permuted(pieces[k], 2 * k, jump)
                swapped[k] = permuted(arrived[k], 1, None)
        return arrived + swapped

    entering = jnp.where(layer == 0, tokens_in, out_grad)
    ids = routes.reshape(layers * micros, tokens)
    both_ids, both_entering = [ids], [entering]
    if paired:
        both_ids.append(permuted(ids, 1, None))
        both_entering.append(permuted(entering, 1, None))
    *pieces, start, order = pl.pallas_call(
        functools.partial(prepare_kernel, (homes, layers, micros, ranks, room, size, count)),
        out_shape=[piece] * count
        + [
            jax.ShapeDtypeStruct((micros - 1, rows, width), bf16),
            jax.ShapeDtypeStruct((2 * micros, rows, homes * rows), bf16),
        ],
        in_specs=[SMEM] + [VMEM] * (2 * homes),
        out_specs=[VMEM] * (count + 2),
        compiler_params=params,
        name="prepare",
    )(places[0], *both_ids, *both_entering)

    def resort(step, arrived):
        entry = step < micros
        ins = list(arrived) + ([start[step - 1]] if entry else [])
        plan = (len(arrived), count, width, micros, entry, last)
        return pl.pallas_call(
            functools.partial(resort_kernel, plan),
            out_shape=[piece] * count,
            in_specs=[SMEM] + [VMEM] * (1 + len(ins)),
            out_specs=[VMEM] * count,
            compiler_params=params,
            name="resort",
        )(places[step], order, *ins)

    own_in, own_out = pl.pallas_call(
        fetch_kernel,
        out_shape=[
            jax.ShapeDtypeStruct(own_in.shape, bf16),
            jax.ShapeDtypeStruct(own_out.shape, bf16),
        ],
        in_specs=[ANY] * 2,
        out_specs=[VMEM] * 2,
        scratch_shapes=[pltpu.SemaphoreType.DMA((2,))],
        compiler_params=params,
        name="fetch",
    )(own_in, own_out)

    def forward(step, arrived, earlier):
        many = len(arrived)
        passes = step <= last
        sent = many if passes else 0
        form = lambda length, dtype: jax.ShapeDtypeStruct((many * size, length), dtype)
        out = pl.pallas_call(
            functools.partial(forward_kernel, many, len(earlier), passes),
            out_shape=[piece] * sent
            + [
                form(width, bf16),
                form(double, f32),
                form(width, bf16),
                form(1, f32),
                form(1, f32),
                form(width, bf16),
                form(inner, bf16),
            ],
            in_specs=[VMEM] * (4 + many) + [ANY] * len(earlier),
            out_specs=[VMEM] * (sent + 7),
            compiler_params=params,
            name="forward",
        )(gain_row, column, own_in, own_out, *arrived, *earlier)
        return out[:sent], out[sent:]

    def record(step, grads, saved, kept):
        sources = sources_of(step, saved)
        operands = [places[step], *grads]
        for group in sources:
            operands += group[5:]
        specs = [SMEM] + [ANY] * (len(operands) - 1)
        aliases = {}
        if kept is not None:
            aliases = {len(operands) + i: i for i in range(4)}
            operands += kept
            specs += [ANY] * 4
        depth = grads[0].shape[0]
        return pl.pallas_call(
            functools.partial(record_kernel, (layers, micros, len(sources), kept is not None)),
            out_shape=[
                jax.ShapeDtypeStruct((micros + 1, depth, length), bf16)
                for length in (width, double, inner, width)
            ],
            in_specs=specs,
            out_specs=[ANY] * 4,
            scratch_shapes=[pltpu.SemaphoreType.DMA((4,))],
            input_output_aliases=aliases,
            compiler_params=params,
            name="record",
        )(*operands)

    def sources_of(step, saved):
        return [
            saved[step - 2 * (last - p)]
            for p in range(layers)
            if 0 <= step - (2 * last - p) < micros
        ]

    bands = 8
    turned_in, turned_out = pl.pallas_call(
        transpose_kernel,
        grid=(bands,),
        out_shape=[
            jax.ShapeDtypeStruct((double, width), bf16),
            jax.ShapeDtypeStruct((width, inner), bf16),
        ],
        in_specs=[
            pl.BlockSpec((width // bands, double), lambda i: (i, 0)),
            pl.BlockSpec((inner, width // bands), lambda i: (0, i)),
        ],
        out_specs=[
            pl.BlockSpec((double, width // bands), lambda i: (0, i)),
            pl.BlockSpec((width // bands, inner), lambda i: (i, 0)),
        ],
        compiler_params=params,
        name="turn",
    )(own_in, own_out)

    def backward(step, arrived, entered, ahead, saved, earlier):
        passes = step + 1 < steps
        many = len(arrived)
        sources = sources_of(step, saved)
        plan = (
            many,
            layers,
            micros,
            len(sources),
            entered is not None,
            step == last,
            len(earlier),
            passes,
        )
        operands = [places[step], gain_row, column, turned_in, turned_out, *arrived]
        if entered is not None:
            operands += entered
        if step == last:
            operands += ahead
        for group in sources:
            operands += group[:5]
        specs = [SMEM] + [VMEM] * (len(operands) - 1) + [ANY] * len(earlier)
        operands += earlier
        sent = many if passes else 0
        out = pl.pallas_call(
            functools.partial(backward_kernel, plan),
            out_shape=[piece] * sent
            + [
                jax.ShapeDtypeStruct((many * size, length), bf16) for length in (double, width)
            ],
            in_specs=specs,
            out_specs=[VMEM] * (sent + 2),
            compiler_params=params,
            name="backward",
        )(*operands)
        return out[:sent], out[sent:]

    arrivals = []
    forwards = [[] for _ in parts]
    kept = [None for _ in parts]
    grads = [None for _ in parts]
    for step in range(steps):
        arrived = to_experts(pieces)
        arrivals.append(arrived)
        pieces, earlier = [None] * count, []
        for index, part in enumerate(parts):
            here = [arrived[k] for k in part]
            passed = None
            if step < last + micros:
                passed, saved = forward(step, here, earlier)
                forwards[index].append(saved)
            if step >= last:
                entered = None
                if step < last + micros:
                    entered = [arrivals[step - last][k] for k in part]
                passed, grads[index] = backward(
                    step, here, entered, passed, forwards[index], earlier
                )
                if step + 1 < steps:
                    kept[index] = record(
                        step, grads[index], forwards[index], kept[index]
                    )
            for k, value in zip(part, passed):
                pieces[k] = value
            earlier = passed[:1]
        if step + 1 == steps:
            break
        if step < last:
            jump = lambda p: (p + 1) % layers
        elif step == last:
            jump = lambda p: p ^ 1
        else:
            jump = lambda p: (p - 1) % layers
        pieces = resort(step + 1, to_homes(pieces, jump))

    cuts = 4
    specs = []
    for part in parts:
        depth = len(part) * size
        column_block = lambda length: pl.BlockSpec((micros, depth, length), lambda i: (0, 0, i))
        whole_block = lambda length: pl.BlockSpec((micros, depth, length), lambda i: (0, 0, 0))
        specs += [
            column_block(width // cuts),
            whole_block(double),
            column_block(inner // cuts),
            whole_block(width),
            pl.BlockSpec((depth, width // cuts), lambda i: (0, i)),
            pl.BlockSpec((depth, double), lambda i: (0, 0)),
            pl.BlockSpec((depth, inner // cuts), lambda i: (0, i)),
            pl.BlockSpec((depth, width), lambda i: (0, 0)),
        ]
    final = []
    for group, pair, saved in zip(kept, grads, forwards):
        normed, activated = saved[steps - 1 - 2 * last][5:]
        final += [*group, normed, pair[0], activated, pair[1]]
    grad_in, grad_out = pl.pallas_call(
        functools.partial(grads_kernel, len(parts)),
        grid=(cuts,),
        out_shape=[
            jax.ShapeDtypeStruct((width, double), bf16),
            jax.ShapeDtypeStruct((inner, width), bf16),
        ],
        in_specs=[SMEM] + specs,
        out_specs=[
            pl.BlockSpec((width // cuts, double), lambda i: (i, 0)),
            pl.BlockSpec((inner // cuts, width), lambda i: (i, 0)),
        ],
        compiler_params=params,
        name="grads",
    )(places[0], *final)
    return grad_in[None, None], grad_out[None, None]


def solution(mesh):
    placed = (
        P(None, "expert", None),
        P(None, "expert", None),
        P(None, None, "expert", None),
        P("pipe", None, None),
        P("pipe", None),
        P("pipe", "expert", None, None),
        P("pipe", "expert", None, None),
    )
    return jax.shard_map(
        shards,
        mesh=mesh,
        in_specs=placed,
        out_specs=(P("pipe", "expert", None, None), P("pipe", "expert", None, None)),
        check_vma=False,
    )
```
